256 devices in a mesh: seq: 32 (over z, x), head: 4 (over y), batch: 2 (over core).
Axes of the slice: x: 4, y: 4, z: 8, core: 2. Of those that a mesh axis runs over, the one named last changes fastest.
Arguments:
- query_states: bfloat16 [16384, 2048], P(('batch', 'seq'), 'head'), parts along dimension 0, may hold values from -8 to 8
- key_states: bfloat16 [16384, 2048], P(('batch', 'seq'), 'head'), parts along dimension 0, may hold values from -8 to 8
- value_states: bfloat16 [16384, 2048], P(('batch', 'seq'), 'head'), parts along dimension 0, may hold values from -6 to 6
- out_grad: bfloat16 [16384, 2048], P(('batch', 'seq'), 'head'), parts along dimension 0, may hold values from -192 to 192
- head_offsets: int32 [16], P('head'), may hold values from 0 to 8191
Outputs:
- query_grad: bfloat16 [16384, 2048], P(('batch', 'seq'), 'head'), parts along dimension 0
- key_grad: bfloat16 [16384, 2048], P(('batch', 'seq'), 'head'), parts along dimension 0
- value_grad: bfloat16 [16384, 2048], P(('batch', 'seq'), 'head'), parts along dimension 0
The draws below stay inside these ranges and needn't reach their ends.
There are 2 independent parts, one for each index of `batch`. The reference program is written for one: setup_inputs(seed, part) draws one part's arguments, and reference() takes and returns one part's arrays. A program takes and returns all parts, laid end to end along the dimension named above; an argument that names none is the same for every part. Nothing has to cross between parts.
All inputs are finite; a program needn't handle non-finite values.
Results may differ from the reference program's by a relative error of at most 0.0056.
Values may be sent and summed in bfloat16 or wider, within the bound.
No kernel may reach another device: no remote copies, remote signals or barrier semaphores. Data moves between devices by JAX's collectives and lax.ppermute only.
A program may use at most 128 MiB of HBM per device.

```python
import jax
import jax.numpy as jnp
from jax import lax

HD = 128
WINDOW = 1024
S_DEV = 256
HEADS = 16
SEQ = 8192
N_SEQ = 32


def paired_fields(key):
    row_total = SEQ
    col_total = HEADS * HD
    key_query = jax.random.fold_in(key, 101)
    key_keys = jax.random.fold_in(key, 102)
    base_query = jnp.clip(jax.random.normal(key_query, (row_total, col_total), jnp.float32), -4.0, 4.0)
    base_keys = jnp.clip(jax.random.normal(key_keys, (row_total, col_total), jnp.float32), -4.0, 4.0)
    return (base_query.astype(jnp.bfloat16), base_keys.astype(jnp.bfloat16))


def draw_query_states(key, part):
    return paired_fields(key)[0]


def draw_key_states(key, part):
    return paired_fields(key)[1]


def place_ends(array, stream_key, low, top_value):
    extent = array.shape
    spot = [jax.random.randint(jax.random.fold_in(stream_key, axis), (), 0, extent[axis]) for axis in range(len(extent))]
    array = array.at[tuple(spot)].set(low)
    longest = extent.index(max(extent))
    spot[longest] = (spot[longest] + 1) % extent[longest]
    return array.at[tuple(spot)].set(top_value)


def level_of(stream_key, shape, shards, low, top_value):
    def one(axis_at, blocks):
        heights = jax.random.uniform(jax.random.fold_in(jax.random.fold_in(stream_key, 6), axis_at), (blocks,), jnp.float32, low / len(shards), top_value / len(shards))
        return jnp.repeat(jnp.exp(heights), shape[axis_at] // blocks).reshape((-1,) + (1,) * (len(shape) - axis_at - 1))

    gain = one(*shards[0])
    for cut in shards[1:]:
        gain = gain * one(*cut)
    return gain


def normal_values(rng, dims, scale, most, cuts=(), kind=jnp.bfloat16):
    entries = scale * jax.random.normal(rng, dims, jnp.float32)
    if cuts:
        entries = entries * level_of(rng, dims, cuts, -0.22, 0.18)
    return jnp.clip(entries, -most, most).astype(kind)


def setup_inputs(seed: int = 0, part: int = 0) -> dict:
    key_list = jax.random.split(jax.random.key(seed), 6)
    part_splits = jax.random.split(jax.random.fold_in(key_list[5], part), 6)
    return {
        "query_states": draw_query_states(jax.random.fold_in(jax.random.fold_in(key_list[5], part), 71), part),
        "key_states": draw_key_states(jax.random.fold_in(jax.random.fold_in(key_list[5], part), 71), part),
        "value_states": normal_values(part_splits[2], (SEQ, HEADS * HD), 1.0, 6.0, ((0, 32), (1, 4))),
        "out_grad": normal_values(part_splits[3], (SEQ, HEADS * HD), 32.0, 192.0, ((0, 32), (1, 4))),
        "head_offsets": place_ends(jax.random.randint(key_list[4], (HEADS,), 0, SEQ), jax.random.fold_in(key_list[4], 1), 0, SEQ - 1).astype(jnp.int32),
    }


masked_score = -1.0e30


def forward_part(queries, keys_in, values_in, allowed, softmax_scale):
    scores = jnp.dot(queries, keys_in.T, preferred_element_type=jnp.float32) * softmax_scale
    scores = jnp.where(allowed, scores, masked_score)
    row_max = jnp.max(scores, axis=-1)
    weights = jnp.exp(scores - row_max[..., None])
    row_sum = jnp.sum(weights, axis=-1)
    row_out = jnp.dot(weights.astype(jnp.bfloat16), values_in, preferred_element_type=jnp.float32)
    return row_max, row_sum, row_out


def backward_part(queries, keys_in, values_in, grads, allowed, log_norm, grad_dot, softmax_scale):
    scores = jnp.dot(queries, keys_in.T, preferred_element_type=jnp.float32) * softmax_scale
    scores = jnp.where(allowed, scores, masked_score)
    weights = jnp.exp(scores - log_norm[..., None])
    grad_values = jnp.dot(weights.astype(jnp.bfloat16).T, grads, preferred_element_type=jnp.float32)
    grad_probs = jnp.dot(grads, values_in.T, preferred_element_type=jnp.float32)
    grad_scores = (weights * (grad_probs - grad_dot[..., None])).astype(jnp.bfloat16)
    grad_queries = jnp.dot(grad_scores, keys_in, preferred_element_type=jnp.float32) * softmax_scale
    grad_keys = jnp.dot(grad_scores.T, queries, preferred_element_type=jnp.float32) * softmax_scale
    return grad_queries, grad_keys, grad_values


def merge_stats(first_stats, second_stats):
    row_max = jnp.maximum(first_stats[0], second_stats[0])
    first_factor = jnp.exp(first_stats[0] - row_max)
    second_factor = jnp.exp(second_stats[0] - row_max)
    row_sum = first_stats[1] * first_factor + second_stats[1] * second_factor
    row_out = first_stats[2] * first_factor[..., None] + second_stats[2] * second_factor[..., None]
    return row_max, row_sum, row_out


def pick_rows(source, stride, first_row):
    shaped = source.reshape((source.shape[0] // stride, stride) + source.shape[1:])
    return lax.dynamic_slice_in_dim(shaped, first_row, 1, axis=1)[:, 0]


def put_rows(source, stride, first_row, update):
    shaped = source.reshape((source.shape[0] // stride, stride) + source.shape[1:])
    return lax.dynamic_update_slice_in_dim(shaped, update[:, None], first_row, axis=1).reshape(source.shape)


def one_head(inputs):
    query, key_rows, value_rows, grad_rows, head_offset = inputs
    softmax_scale = HD ** -0.5
    reach_slabs = WINDOW // S_DEV
    span_cols = (reach_slabs + 1) * S_DEV
    padding = jnp.zeros((reach_slabs * S_DEV, HD), jnp.bfloat16)
    key_pad = jnp.concatenate([padding, key_rows], axis=0)
    value_pad = jnp.concatenate([padding, value_rows], axis=0)
    local_rows = jnp.arange(S_DEV, dtype=jnp.int32)[:, None]
    key_cols = jnp.arange(span_cols, dtype=jnp.int32)[None, :]
    distance = local_rows - key_cols + reach_slabs * S_DEV

    def near_inputs(slab_index):
        first_row = (slab_index * S_DEV).astype(jnp.int32)
        allowed = (distance >= 0) & (distance < WINDOW) & (first_row + key_cols - reach_slabs * S_DEV >= 0)
        return (lax.dynamic_slice_in_dim(query, first_row, S_DEV),
                lax.dynamic_slice_in_dim(key_pad, first_row, span_cols),
                lax.dynamic_slice_in_dim(value_pad, first_row, span_cols),
                lax.dynamic_slice_in_dim(grad_rows, first_row, S_DEV),
                allowed, first_row)

    def near_forward(slab_index):
        q_part, k_part, v_part, g_part, allowed, first_row = near_inputs(slab_index)
        return forward_part(q_part, k_part, v_part, allowed, softmax_scale)

    slab_list = jnp.arange(N_SEQ, dtype=jnp.int32)
    row_max, row_sum, row_out = lax.map(near_forward, slab_list)
    stats = (row_max.reshape(SEQ), row_sum.reshape(SEQ), row_out.reshape(SEQ, HD))
    level_count = N_SEQ.bit_length() - 1
    causal = jnp.arange(S_DEV, dtype=jnp.int32)[None, :] <= jnp.arange(S_DEV, dtype=jnp.int32)[:, None]
    for level_num in range(1, level_count + 1):
        stride = 2 ** level_num
        first_row = (head_offset % stride).astype(jnp.int32)
        segments = N_SEQ // stride
        sparse_q = pick_rows(query, stride, first_row).reshape(segments, S_DEV, HD)
        sparse_k = pick_rows(key_rows, stride, first_row).reshape(segments, S_DEV, HD)
        sparse_v = pick_rows(value_rows, stride, first_row).reshape(segments, S_DEV, HD)
        update = jax.vmap(forward_part, in_axes=(0, 0, 0, None, None))(sparse_q, sparse_k, sparse_v, causal, softmax_scale)
        update = (update[0].reshape(-1), update[1].reshape(-1), update[2].reshape(-1, HD))
        current = tuple(pick_rows(member, stride, first_row) for member in stats)
        merged = merge_stats(current, update)
        stats = tuple(put_rows(member, stride, first_row, fresh) for member, fresh in zip(stats, merged))
    log_norm = stats[0] + jnp.log(stats[1])
    out_rows = stats[2] / stats[1][:, None]
    grad_dot = jnp.sum(grad_rows.astype(jnp.float32) * out_rows, axis=-1)

    def near_backward(slab_index):
        q_part, k_part, v_part, g_part, allowed, first_row = near_inputs(slab_index)
        return backward_part(q_part, k_part, v_part, g_part, allowed,
                             lax.dynamic_slice_in_dim(log_norm, first_row, S_DEV),
                             lax.dynamic_slice_in_dim(grad_dot, first_row, S_DEV), softmax_scale)

    grad_query, near_key, near_value = lax.map(near_backward, slab_list)
    grad_query = grad_query.reshape(SEQ, HD)
    near_key = near_key.reshape(N_SEQ, reach_slabs + 1, S_DEV, HD)
    near_value = near_value.reshape(N_SEQ, reach_slabs + 1, S_DEV, HD)
    grad_key = jnp.zeros((N_SEQ, S_DEV, HD), jnp.float32)
    grad_value = jnp.zeros((N_SEQ, S_DEV, HD), jnp.float32)
    for block_index in range(reach_slabs + 1):
        behind = reach_slabs - block_index
        if behind < N_SEQ:
            grad_key = grad_key + jnp.pad(near_key[behind:, block_index], ((0, behind), (0, 0), (0, 0)))
            grad_value = grad_value + jnp.pad(near_value[behind:, block_index], ((0, behind), (0, 0), (0, 0)))
    grad_key = grad_key.reshape(SEQ, HD)
    grad_value = grad_value.reshape(SEQ, HD)
    for level_num in range(1, level_count + 1):
        stride = 2 ** level_num
        first_row = (head_offset % stride).astype(jnp.int32)
        segments = N_SEQ // stride
        sparse_q = pick_rows(query, stride, first_row).reshape(segments, S_DEV, HD)
        sparse_k = pick_rows(key_rows, stride, first_row).reshape(segments, S_DEV, HD)
        sparse_v = pick_rows(value_rows, stride, first_row).reshape(segments, S_DEV, HD)
        sparse_g = pick_rows(grad_rows, stride, first_row).reshape(segments, S_DEV, HD)
        sparse_norm = pick_rows(log_norm, stride, first_row).reshape(segments, S_DEV)
        sparse_dot = pick_rows(grad_dot, stride, first_row).reshape(segments, S_DEV)
        level_query, level_key, level_value = jax.vmap(backward_part, in_axes=(0, 0, 0, 0, None, 0, 0, None))(
            sparse_q, sparse_k, sparse_v, sparse_g, causal, sparse_norm, sparse_dot, softmax_scale)
        grad_query = put_rows(grad_query, stride, first_row, pick_rows(grad_query, stride, first_row) + level_query.reshape(-1, HD))
        grad_key = put_rows(grad_key, stride, first_row, pick_rows(grad_key, stride, first_row) + level_key.reshape(-1, HD))
        grad_value = put_rows(grad_value, stride, first_row, pick_rows(grad_value, stride, first_row) + level_value.reshape(-1, HD))
    return grad_query, grad_key, grad_value


def reference(query_states, key_states, value_states, out_grad, head_offsets):
    def split_heads(source):
        return source.reshape(SEQ, HEADS, HD).transpose(1, 0, 2)

    def join_heads(source):
        return source.transpose(1, 0, 2).reshape(SEQ, HEADS * HD).astype(jnp.bfloat16)

    grad_query, grad_key, grad_value = lax.map(one_head, (split_heads(query_states), split_heads(key_states),
                                                         split_heads(value_states), split_heads(out_grad), head_offsets))
    return join_heads(grad_query), join_heads(grad_key), join_heads(grad_value)
```

```python
import functools

import jax
import jax.numpy as jnp
from jax import lax
from jax.experimental import pallas as pl
from jax.experimental.pallas import tpu as pltpu
from jax.sharding import PartitionSpec as P

COLS = 4
SLAB = 256
HD = 128
ROW = COLS * SLAB
SPAN = ROW + SLAB
NEG = -1e30
SCALE = HD**-0.5
LOG2E = 1.4426950408889634
FAR8 = ROW // 8
FAR16 = ROW // 16
FARK = FAR8 + 6 * FAR16
F32 = jnp.float32
BF16 = jnp.bfloat16


def across(value, step, planes):
    pairs = [
        (p * COLS + c, p * COLS + (c + step) % COLS) for p in range(planes) for c in range(COLS)
    ]
    return lax.ppermute(value, "seq", pairs)


def along(value, step, planes):
    pairs = [
        (p * COLS + c, (p + step) * COLS + c)
        for p in range(planes)
        for c in range(COLS)
        if 0 <= p + step < planes
    ]
    return lax.ppermute(value, "seq", pairs)


def place():
    pos = lax.axis_index("seq")
    return pos // COLS, pos % COLS


def mm(left, right, dims):
    return lax.dot_general(left, right, (dims, ((), ())), preferred_element_type=F32)


def nn(left, right):
    return mm(left, right, ((1,), (0,)))


def nt(left, right):
    return mm(left, right, ((1,), (1,)))


def tn(left, right):
    return mm(left, right, ((0,), (0,)))


def call(kernel, out, scratch=(), flops=1000000, smem=(), nin=0):
    specs = [
        pl.BlockSpec(memory_space=pltpu.SMEM if i in smem else pltpu.VMEM) for i in range(nin)
    ]
    return pl.pallas_call(
        kernel,
        out_shape=out,
        in_specs=specs,
        out_specs=jax.tree.map(lambda _: pl.BlockSpec(memory_space=pltpu.VMEM), out),
        scratch_shapes=scratch,
        compiler_params=pltpu.CompilerParams(vmem_limit_bytes=48 << 20),
        cost_estimate=pl.CostEstimate(flops=flops, bytes_accessed=2 << 20, transcendentals=0),
    )


def pack_kernel(one_ref, two_ref, *out_refs):
    _, col = place()
    for step in range(COLS):
        lanes = pl.ds(pl.multiple_of(((col + step) % COLS) * HD, HD), HD)
        out_refs[step][0] = one_ref[:, lanes]
        out_refs[step][1] = two_ref[:, lanes]


def pack(one, two):
    piece = jax.ShapeDtypeStruct((2, SLAB, HD), BF16)
    return call(pack_kernel, [piece] * COLS, nin=2)(one, two)


def pick(stride, rest, rows, width):
    r = lax.broadcasted_iota(jnp.int32, (rows, width), 0)
    c = lax.broadcasted_iota(jnp.int32, (rows, width), 1)
    return (c == r * stride + rest).astype(BF16)


def thin_kernel(off_ref, *refs):
    _, col = place()
    chosen = pick(16, off_ref[col] % 16, SLAB // 16, SLAB)
    out_ref = refs[COLS]
    for step in range(COLS):
        rows = pl.ds(pl.multiple_of(((col - step + COLS) % COLS) * (SLAB // 16), 16), SLAB // 16)
        for which in range(2):
            out_ref[which, rows] = nn(chosen, refs[step][which]).astype(BF16)


def thin(offsets, pieces):
    out = jax.ShapeDtypeStruct((2, FAR16, HD), BF16)
    return call(thin_kernel, out, smem=(0,), nin=1 + COLS)(offsets, *pieces)


def depth_of(index, off):
    rest = (index - off + 32768) % 32
    total = jnp.zeros(index.shape, F32)
    for level in range(1, 6):
        total = total + (rest % (2**level) == 0).astype(F32)
    return total


def main_kernel(*refs):
    off_ref = refs[0]
    kv = refs[1:5]
    qg = refs[5:9]
    pv = refs[9:13]
    g2_ref, g4_ref, g6_ref = refs[13:16]
    dq_out = refs[16:20]
    prev_out, h2_ref, h4_ref, h6_ref, own_ref = refs[20:25]
    (kk, vv, qq, gg, sc, ctab, m_b, l_b, o_b, d_b, dq, dk, dv, kf, vf) = refs[25:]
    plane, col = place()
    off = off_ref[col]
    for step in range(COLS):
        slab = (col - step + COLS) % COLS
        rows = pl.ds(pl.multiple_of(slab * SLAB, SLAB), SLAB)
        late = pl.ds(pl.multiple_of(slab * SLAB + ROW, SLAB), SLAB)
        kk[late] = kv[step][0]
        vv[late] = kv[step][1]
        kk[rows] = pv[step][0]
        vv[rows] = pv[step][1]
        qq[rows] = qg[step][0]
        gg[rows] = qg[step][1]

    deep_q = depth_of(lax.broadcasted_iota(jnp.int32, (SLAB, SLAB), 0), off)
    deep_k = depth_of(lax.broadcasted_iota(jnp.int32, (SLAB, SLAB), 1), off)
    both = jnp.minimum(deep_q, deep_k)
    ctab[0] = jnp.ones((SLAB, SLAB), F32)
    ctab[1] = 1.0 + jnp.maximum(both - 1.0, 0.0)
    ctab[2] = 1.0 + both

    rest8 = off % 8
    thin8 = pick(8, rest8, SLAB // 8, SLAB)

    def thinned(ref):
        parts = [nn(thin8, ref[pl.ds(b * SLAB, SLAB), :]) for b in range(COLS)]
        return jnp.concatenate(parts, axis=0).astype(BF16)

    kf[pl.ds(0, FAR8)] = thinned(kk)
    vf[pl.ds(0, FAR8)] = thinned(vv)
    for i, g_ref in enumerate((g2_ref, g4_ref, g6_ref)):
        for j in range(2):
            rows = pl.ds(FAR8 + (2 * i + j) * FAR16, FAR16)
            kf[rows] = g_ref[j, 0]
            vf[rows] = g_ref[j, 1]
    qs = thinned(qq)
    gs = thinned(gg)
    c = lax.broadcasted_iota(jnp.int32, (FAR8, FARK), 1)
    r = lax.broadcasted_iota(jnp.int32, (FAR8, FARK), 0)
    far = c - FAR8
    back = jnp.where(c < FAR8, 1, 2 + far // FAR16)
    spot = jnp.where(c < FAR8, c * 8 + rest8, (far % FAR16) * 16 + off % 16)
    other = plane - back
    first = jnp.where(
        other < 0,
        9,
        jnp.where(other // 2 == plane // 2, 3, jnp.where(other // 4 == plane // 4, 4, 5)),
    )
    deep = jnp.minimum(depth_of(r * 8 + rest8, off), depth_of(spot, off))
    times = jnp.maximum(deep - first.astype(F32) + 1.0, 0.0)
    s_far = jnp.where(times > 0.0, nt(qs, kf[...]), NEG)
    m_far = jnp.max(s_far, axis=1, keepdims=True)
    e_far = jnp.exp2((s_far - m_far) * (SCALE * LOG2E)) * times
    l_far = jnp.sum(e_far, axis=1, keepdims=True)
    o_far = nn(e_far.astype(BF16), vf[...])
    strided = pl.ds(rest8, FAR8, stride=8)
    m_b[...] = jnp.full((ROW, HD), NEG, F32)
    l_b[...] = jnp.zeros((ROW, HD), F32)
    o_b[...] = jnp.zeros((ROW, HD), F32)
    m_b[strided, :] = jnp.broadcast_to(m_far, (FAR8, HD))
    l_b[strided, :] = jnp.broadcast_to(l_far, (FAR8, HD))
    o_b[strided, :] = o_far
    dk[...] = jnp.zeros((2 * ROW, HD), F32)
    dv[...] = jnp.zeros((2 * ROW, HD), F32)
    lost = jnp.where(plane > 0, 0.0, NEG)

    def block(qb, carry):
        rows = pl.ds(pl.multiple_of(qb * SLAB, SLAB), SLAB)
        q = qq[rows]
        g = gg[rows]
        i = lax.broadcasted_iota(jnp.int32, (SLAB, SLAB), 0)
        j = lax.broadcasted_iota(jnp.int32, (SLAB, SLAB), 1)
        m_old = m_b[rows][:, :1]
        m = m_old
        for b in range(COLS + 1):
            cols = pl.ds(pl.multiple_of((qb + b) * SLAB, SLAB), SLAB)
            s = nt(q, kk[cols])
            if b < COLS:
                s = s + jnp.where(qb + b < COLS, lost, 0.0)
            if b == 0:
                s = jnp.where(j > i, s, NEG)
            if b == COLS:
                s = jnp.where(j <= i, s, NEG)
            sc[b] = s
            m = jnp.maximum(m, jnp.max(s, axis=1, keepdims=True))
        fade = jnp.exp2((m_old - m) * (SCALE * LOG2E))
        total = l_b[rows][:, :1] * fade
        out = o_b[rows] * fade
        for b in range(COLS + 1):
            cols = pl.ds(pl.multiple_of((qb + b) * SLAB, SLAB), SLAB)
            e = jnp.exp2((sc[b] - m) * (SCALE * LOG2E))
            if b > 0:
                same = (qb + b - COLS) // 2 == qb // 2
                e = e * ctab[jnp.where(qb + b < COLS, 0, jnp.where(same, 2, 1))]
            sc[b] = e
            total = total + jnp.sum(e, axis=1, keepdims=True)
            out = out + nn(e.astype(BF16), vv[cols])
        inv = 1.0 / total
        dot = jnp.sum(g.astype(F32) * out, axis=1, keepdims=True) * inv
        m_b[rows] = jnp.broadcast_to(m, (SLAB, HD))
        l_b[rows] = jnp.broadcast_to(inv, (SLAB, HD))
        d_b[rows] = jnp.broadcast_to(dot, (SLAB, HD))
        dq_acc = jnp.zeros((SLAB, HD), F32)
        for b in range(COLS + 1):
            cols = pl.ds(pl.multiple_of((qb + b) * SLAB, SLAB), SLAB)
            p = sc[b] * inv
            dv[cols] += tn(p.astype(BF16), g)
            ds = (p * (nt(g, vv[cols]) - dot)).astype(BF16)
            dq_acc = dq_acc + nn(ds, kk[cols])
            dk[cols] += tn(ds, q)
        dq[rows] = dq_acc
        return carry

    lax.fori_loop(0, COLS, block, 0)

    m_s = m_b[strided, :][:, :1]
    i_s = l_b[strided, :][:, :1]
    d_s = d_b[strided, :][:, :1]
    p = jnp.exp2((s_far - m_s) * (SCALE * LOG2E)) * times * i_s
    ds = (p * (nt(gs, vf[...]) - d_s)).astype(BF16)
    dk_far = tn(ds, qs)
    dv_far = tn(p.astype(BF16), gs)
    dq[strided, :] = dq[strided, :] + nn(ds, kf[...])
    dk[strided, :] = dk[strided, :] + dk_far[:FAR8]
    dv[strided, :] = dv[strided, :] + dv_far[:FAR8]
    for i, h_ref in enumerate((h2_ref, h4_ref, h6_ref)):
        for j in range(2):
            lo = FAR8 + (2 * i + j) * FAR16
            h_ref[j, 0] = dk_far[lo : lo + FAR16].astype(BF16)
            h_ref[j, 1] = dv_far[lo : lo + FAR16].astype(BF16)
    prev_out[0] = dk[pl.ds(0, ROW), :].astype(BF16)
    prev_out[1] = dv[pl.ds(0, ROW), :].astype(BF16)
    own_ref[0] = dk[pl.ds(ROW, ROW), :]
    own_ref[1] = dv[pl.ds(ROW, ROW), :]
    for step in range(COLS):
        rows = pl.ds(pl.multiple_of(((col + step) % COLS) * SLAB, SLAB), SLAB)
        dq_out[step][...] = (dq[rows] * SCALE).astype(BF16)


def main(offsets, kv, qg, pv, far):
    part = jax.ShapeDtypeStruct((SLAB, HD), BF16)
    pair = jax.ShapeDtypeStruct((2, 2, FAR16, HD), BF16)
    out = [part] * COLS + [
        jax.ShapeDtypeStruct((2, ROW, HD), BF16),
        pair,
        pair,
        pair,
        jax.ShapeDtypeStruct((2, ROW, HD), F32),
    ]
    scratch = [
        pltpu.VMEM((2 * ROW, HD), BF16),
        pltpu.VMEM((2 * ROW, HD), BF16),
        pltpu.VMEM((ROW, HD), BF16),
        pltpu.VMEM((ROW, HD), BF16),
        pltpu.VMEM((COLS + 1, SLAB, SLAB), F32),
        pltpu.VMEM((3, SLAB, SLAB), F32),
        pltpu.VMEM((ROW, HD), F32),
        pltpu.VMEM((ROW, HD), F32),
        pltpu.VMEM((ROW, HD), F32),
        pltpu.VMEM((ROW, HD), F32),
        pltpu.VMEM((ROW, HD), F32),
        pltpu.VMEM((2 * ROW, HD), F32),
        pltpu.VMEM((2 * ROW, HD), F32),
        pltpu.VMEM((FARK, HD), BF16),
        pltpu.VMEM((FARK, HD), BF16),
    ]
    return call(main_kernel, out, scratch, flops=2000000000, smem=(0,), nin=16)(
        offsets, *kv, *qg, *pv, *far
    )


def join_kernel(off_ref, own_ref, near_ref, a2_ref, a4_ref, a6_ref, b1_ref, *refs):
    out = refs[:COLS]
    acc = refs[COLS]
    _, col = place()
    strided = pl.ds(off_ref[col] % 16, FAR16, stride=16)
    for which in range(2):
        acc[...] = own_ref[which] + near_ref[which].astype(F32)
        extra = b1_ref[which].astype(F32)
        for ref in (a2_ref, a4_ref, a6_ref):
            extra = extra + ref[0, which].astype(F32)
        acc[strided, :] = acc[strided, :] + extra
        for step in range(COLS):
            rows = pl.ds(pl.multiple_of(((col + step) % COLS) * SLAB, SLAB), SLAB)
            value = acc[rows]
            if which == 0:
                value = value * SCALE
            out[step][which] = value.astype(BF16)


def join(offsets, own, near, a2, a4, a6, b1):
    piece = jax.ShapeDtypeStruct((2, SLAB, HD), BF16)
    return call(
        join_kernel, [piece] * COLS, [pltpu.VMEM((ROW, HD), F32)], smem=(0,), nin=7
    )(offsets, own, near, a2, a4, a6, b1)


def spread_kernel(*refs):
    dq_in = refs[:COLS]
    kv_in = refs[COLS : 2 * COLS]
    q_ref, k_ref, v_ref = refs[2 * COLS :]
    _, col = place()
    for step in range(COLS):
        lanes = pl.ds(pl.multiple_of(((col - step + COLS) % COLS) * HD, HD), HD)
        q_ref[:, lanes] = dq_in[step][...]
        k_ref[:, lanes] = kv_in[step][0]
        v_ref[:, lanes] = kv_in[step][1]


def spread(dq, dkv):
    out = jax.ShapeDtypeStruct((SLAB, COLS * HD), BF16)
    return call(spread_kernel, [out] * 3, nin=2 * COLS)(*dq, *dkv)


def body(planes, query_states, key_states, value_states, out_grad, head_offsets):
    def exchange(pieces):
        return [pieces[0]] + [across(pieces[s], s, planes) for s in range(1, COLS)]

    kv = exchange(pack(key_states, value_states))
    qg = exchange(pack(query_states, out_grad))
    pv = [along(piece, 1, planes) for piece in kv]
    mine = thin(head_offsets, kv)
    pair = jnp.stack([mine, along(mine, 1, planes)])
    far = [along(pair, step, planes) for step in (2, 4, 6)]
    results = main(head_offsets, kv, qg, pv, far)
    dq = exchange(results[:COLS])
    near, h2, h4, h6, own = results[COLS:]
    near = along(near, -1, planes)
    a2, a4, a6 = [along(h, -step, planes) for h, step in ((h2, 2), (h4, 4), (h6, 6))]
    older = (a2[1].astype(F32) + a4[1].astype(F32) + a6[1].astype(F32)).astype(BF16)
    b1 = along(older, -1, planes)
    dkv = exchange(join(head_offsets, own, near, a2, a4, a6, b1))
    return tuple(spread(dq, dkv))


def solution(mesh):
    spec = P(("batch", "seq"), "head")
    planes = mesh.shape["seq"] // COLS
    return jax.shard_map(
        functools.partial(body, planes),
        mesh=mesh,
        in_specs=(spec, spec, spec, spec, P("head")),
        out_specs=(spec, spec, spec),
        check_vma=False,
    )
```

```python
import functools

import jax
import jax.numpy as jnp
from jax import lax
from jax.experimental import pallas as pl
from jax.experimental.pallas import tpu as pltpu
from jax.sharding import PartitionSpec as P

COLS = 4
SLAB = 256
HD = 128
ROW = COLS * SLAB
NEG = -1e30
SCALE = HD**-0.5
LOG2E = 1.4426950408889634
FAR8 = ROW // 8
FAR16 = ROW // 16
FAR32 = ROW // 32
FARK = FAR8 + 2 * FAR16 + 4 * FAR32
C2 = SCALE * LOG2E
F32 = jnp.float32
BF16 = jnp.bfloat16


def across(value, step, planes):
    pairs = [
        (p * COLS + c, p * COLS + (c + step) % COLS) for p in range(planes) for c in range(COLS)
    ]
    return lax.ppermute(value, "seq", pairs)


def along(value, step, planes):
    pairs = [
        (p * COLS + c, (p + step) % planes * COLS + c) for p in range(planes) for c in range(COLS)
    ]
    return lax.ppermute(value, "seq", pairs)


def place():
    pos = lax.axis_index("seq")
    return pos // COLS, pos % COLS


def mm(left, right, dims):
    return lax.dot_general(left, right, (dims, ((), ())), preferred_element_type=F32)


def nn(left, right):
    return mm(left, right, ((1,), (0,)))


def nt(left, right):
    return mm(left, right, ((1,), (1,)))


def tn(left, right):
    return mm(left, right, ((0,), (0,)))


def call(kernel, out, scratch=(), smem=(), nin=0):
    here = pltpu.VMEM
    specs = [pl.BlockSpec(memory_space=pltpu.SMEM if i in smem else here) for i in range(nin)]
    return pl.pallas_call(
        kernel,
        out_shape=out,
        in_specs=specs,
        out_specs=jax.tree.map(lambda _: pl.BlockSpec(memory_space=here), out),
        scratch_shapes=scratch,
        compiler_params=pltpu.CompilerParams(vmem_limit_bytes=24 << 20),
        cost_estimate=pl.CostEstimate(flops=1, bytes_accessed=1, transcendentals=0),
    )


def pack_kernel(one_ref, two_ref, *out_refs):
    _, col = place()
    for step in range(COLS):
        lanes = pl.ds(pl.multiple_of(((col + step) % COLS) * HD, HD), HD)
        out_refs[step][0] = one_ref[:, lanes]
        out_refs[step][1] = two_ref[:, lanes]


def pack(one, two):
    piece = jax.ShapeDtypeStruct((2, SLAB, HD), BF16)
    return call(pack_kernel, [piece] * COLS, nin=2)(one, two)


def pick(stride, rest, rows, width):
    r = lax.broadcasted_iota(jnp.int32, (rows, width), 0)
    c = lax.broadcasted_iota(jnp.int32, (rows, width), 1)
    return (c == r * stride + rest).astype(BF16)


def rows_of(block):
    return pl.ds(block * SLAB, SLAB)


def stack_kernel(*refs):
    _, col = place()
    row_ref = refs[COLS]
    for step in range(COLS):
        slab = (col - step + COLS) % COLS
        rows = pl.ds(pl.multiple_of(slab * SLAB, SLAB), SLAB)
        for which in range(2):
            row_ref[which, rows] = refs[step][which]


def stack(pieces):
    return call(stack_kernel, jax.ShapeDtypeStruct((2, ROW, HD), BF16), nin=COLS)(*pieces)


def pair_kernel(off_ref, mine_ref, back_ref, wide_ref, slim_ref):
    _, col = place()
    off = off_ref[col]
    by16 = pick(16, off % 16, SLAB // 16, SLAB)
    by32 = pick(32, off % 32, SLAB // 32, SLAB)
    for j, ref in enumerate((mine_ref, back_ref)):
        for which in range(2):
            wide = [nn(by16, ref[which, rows_of(b)]) for b in range(COLS)]
            slim = [nn(by32, ref[which, rows_of(b)]) for b in range(COLS)]
            wide_ref[j, which] = jnp.concatenate(wide, axis=0).astype(BF16)
            slim_ref[j, which] = jnp.concatenate(slim, axis=0).astype(BF16)


def pair_up(offsets, mine, back):
    out = [
        jax.ShapeDtypeStruct((2, 2, FAR16, HD), BF16),
        jax.ShapeDtypeStruct((2, 2, FAR32, HD), BF16),
    ]
    return call(pair_kernel, out, smem=(0,), nin=3)(offsets, mine, back)


def depth_of(index, off):
    rest = (index - off) & 31
    total = jnp.zeros(index.shape, F32)
    for level in range(1, 6):
        total = total + ((rest & (2**level - 1)) == 0).astype(F32)
    return total


def iota(shape, axis):
    return lax.broadcasted_iota(jnp.int32, shape, axis)


def thinned(thin8, from_ref, few_ref):
    for which in range(2):
        for b in range(COLS):
            rows = pl.ds(b * (SLAB // 8), SLAB // 8)
            few_ref[which, rows] = nn(thin8, from_ref[which, rows_of(b)]).astype(BF16)


def first_own_kernel(off_ref, kv_ref, *refs):
    qg = refs[:COLS]
    stat_ref, qg_ref, tab_ref, few_ref, sc = refs[COLS:]
    _, col = place()
    off = off_ref[col]
    thin8 = pick(8, off % 8, SLAB // 8, SLAB)
    for step in range(COLS):
        slab = (col - step + COLS) % COLS
        rows = pl.ds(pl.multiple_of(slab * SLAB, SLAB), SLAB)
        for which in range(2):
            qg_ref[which, rows] = qg[step][which]
    thinned(thin8, qg_ref, few_ref)
    deep_k = depth_of(iota((SLAB, HD), 0), off)
    deep_k = jnp.concatenate([deep_k, deep_k], axis=1)
    deep_q = depth_of(iota((8, SLAB), 1), off)[:1]
    both = jnp.minimum(deep_k, deep_q)
    tab_ref[0] = 1.0 + jnp.maximum(both - 1.0, 0.0)
    tab_ref[1] = 1.0 + both
    stat_ref[...] = jnp.zeros((8, ROW), F32)
    seen = iota((SLAB, SLAB), 0) <= iota((SLAB, SLAB), 1)
    for qb in range(COLS):
        q = qg_ref[0, rows_of(qb)]
        g = qg_ref[1, rows_of(qb)]
        m = None
        for kb in range(qb + 1):
            s = nt(kv_ref[0, rows_of(kb)], q) * C2
            if kb == qb:
                s = jnp.where(seen, s, NEG)
            sc[rows_of(kb)] = s
            top = jnp.max(s, axis=0, keepdims=True)
            m = top if m is None else jnp.maximum(m, top)
        total = jnp.zeros((1, SLAB), F32)
        dot = jnp.zeros((1, SLAB), F32)
        for kb in range(qb + 1):
            e = jnp.exp2(sc[rows_of(kb)] - m)
            dp = nt(kv_ref[1, rows_of(kb)], g) * tab_ref[int(kb // 2 == qb // 2)]
            total = total + jnp.sum(
                e * tab_ref[int(kb // 2 == qb // 2)], axis=0, keepdims=True
            )
            dot = dot + jnp.sum(e.astype(BF16).astype(F32) * dp, axis=0, keepdims=True)
        lanes = pl.ds(qb * SLAB, SLAB)
        stat_ref[0:1, lanes] = m
        stat_ref[1:2, lanes] = total
        stat_ref[2:3, lanes] = dot


def first_own(offsets, kv, qg):
    out = [
        jax.ShapeDtypeStruct((8, ROW), F32),
        jax.ShapeDtypeStruct((2, ROW, HD), BF16),
        jax.ShapeDtypeStruct((2, SLAB, SLAB), F32),
        jax.ShapeDtypeStruct((2, FAR8, HD), BF16),
    ]
    scratch = [pltpu.VMEM((ROW, SLAB), F32)]
    return call(first_own_kernel, out, scratch, smem=(0,), nin=2 + COLS)(
        offsets, kv, *qg
    )


def first_prev_kernel(
    off_ref, kv_ref, qg_ref, so_ref, stat_ref, some_ref, few_ref, sc
):
    plane, col = place()
    rest8 = off_ref[col] % 8
    thinned(pick(8, rest8, SLAB // 8, SLAB), kv_ref, few_ref)
    there = plane > 0
    stat_ref[...] = jnp.zeros((8, ROW), F32)
    seen = iota((SLAB, SLAB), 0) > iota((SLAB, SLAB), 1)
    for qb in range(COLS):
        q = qg_ref[0, rows_of(qb)]
        g = qg_ref[1, rows_of(qb)]
        m = None
        for kb in range(qb, COLS):
            s = nt(kv_ref[0, rows_of(kb)], q) * C2
            if kb == qb:
                s = jnp.where(seen, s, NEG)
            sc[rows_of(kb)] = s
            top = jnp.max(s, axis=0, keepdims=True)
            m = top if m is None else jnp.maximum(m, top)
        total = jnp.zeros((1, SLAB), F32)
        dot = jnp.zeros((1, SLAB), F32)
        for kb in range(qb, COLS):
            s = sc[rows_of(kb)]
            e = jnp.exp2(s - m)
            if kb == qb:
                e = jnp.where(seen, e, 0.0)
            total = total + jnp.sum(e, axis=0, keepdims=True)
            dp = nt(kv_ref[1, rows_of(kb)], g)
            dot = dot + jnp.sum(e.astype(BF16).astype(F32) * dp, axis=0, keepdims=True)
        lanes = pl.ds(qb * SLAB, SLAB)
        mp = jnp.where(there, m, NEG)
        mo = so_ref[0:1, lanes]
        m = jnp.maximum(mo, mp)
        fo = jnp.exp2(mo - m)
        fp = jnp.where(there, jnp.exp2(mp - m), 0.0)
        stat_ref[0:1, lanes] = m
        stat_ref[1:2, lanes] = so_ref[1:2, lanes] * fo + total * fp
        stat_ref[2:3, lanes] = so_ref[2:3, lanes] * fo + dot * fp
    some_ref[...] = lax.dot_general(
        stat_ref[...], every8(rest8), (((1,), (1,)), ((), ())),
        precision=lax.Precision.HIGHEST, preferred_element_type=F32,
    )


def every8(rest8):
    return (iota((FAR8, ROW), 1) == iota((FAR8, ROW), 0) * 8 + rest8).astype(F32)


def first_prev(offsets, kv, qg, stat_own):
    out = [
        jax.ShapeDtypeStruct((8, ROW), F32),
        jax.ShapeDtypeStruct((8, FAR8), F32),
        jax.ShapeDtypeStruct((2, FAR8, HD), BF16),
    ]
    scratch = [pltpu.VMEM((ROW, SLAB), F32)]
    return call(first_prev_kernel, out, scratch, smem=(0,), nin=4)(
        offsets, kv, qg, stat_own
    )


def far_kernel(
    off_ref, kv8_ref, qg8_ref, g2_ref, g4_ref, g6_ref, stat_ref, some_ref,
    fin_ref, h2_ref, h4_ref, h6_ref, dqf_ref, pf_ref, kf, vf, near,
):
    plane, col = place()
    off = off_ref[col]
    rest8 = off % 8
    kf[pl.ds(0, FAR8)] = kv8_ref[0]
    vf[pl.ds(0, FAR8)] = kv8_ref[1]
    lo = FAR8
    for ref, size in ((g2_ref, FAR16), (g4_ref, FAR32), (g6_ref, FAR32)):
        for j in range(2):
            kf[pl.ds(lo, size)] = ref[j, 0]
            vf[pl.ds(lo, size)] = ref[j, 1]
            lo += size
    qs = qg8_ref[0]
    gs = qg8_ref[1]
    r = iota((FARK, HD), 0)
    mid = r - FAR8
    end = mid - 2 * FAR16
    back = jnp.where(r < FAR8, 1, jnp.where(end < 0, 2 + mid // FAR16, 4 + end // FAR32))
    spot = jnp.where(
        r < FAR8,
        r * 8 + rest8,
        jnp.where(end < 0, (mid % FAR16) * 16 + off % 16, (end % FAR32) * 32 + off % 32),
    )
    other = plane - back
    first = jnp.where(
        other < 0,
        9,
        jnp.where(other // 2 == plane // 2, 3, jnp.where(other // 4 == plane // 4, 4, 5)),
    )
    deep_q = depth_of(iota((8, FAR8), 1) * 8 + rest8, off)[:1]
    deep = jnp.minimum(deep_q, depth_of(spot, off))
    times = jnp.maximum(deep - first.astype(F32) + 1.0, 0.0)
    s = jnp.where(times > 0.0, nt(kf[...], qs) * C2, NEG)
    dp = nt(vf[...], gs)
    m_f = jnp.max(s, axis=0, keepdims=True)
    e = jnp.exp2(s - m_f)
    l_f = jnp.sum(e * times, axis=0, keepdims=True)
    d_f = jnp.sum(e.astype(BF16).astype(F32) * (dp * times), axis=0, keepdims=True)

    m_n, l_n, d_n = some_ref[0:1], some_ref[1:2], some_ref[2:3]
    m_s = jnp.maximum(m_n, m_f)
    fn = jnp.exp2(m_n - m_s)
    ff = jnp.exp2(m_f - m_s)
    l_s = l_n * fn + l_f * ff
    log_s = m_s + jnp.log2(l_s)
    dot_s = (d_n * fn + d_f * ff) / l_s
    near[...] = jnp.zeros((8, FAR8), F32)
    near[0:1] = log_s
    near[1:2] = dot_s
    wide = lax.dot_general(
        near[...], every8(rest8), (((1,), (0,)), ((), ())),
        precision=lax.Precision.HIGHEST, preferred_element_type=F32,
    )
    hit = (iota((8, ROW), 1) % 8 == rest8)[:1]
    fin_ref[...] = jnp.zeros((8, ROW), F32)
    total = stat_ref[1:2]
    fin_ref[0:1] = jnp.where(hit, wide[0:1], stat_ref[0:1] + jnp.log2(total))
    fin_ref[1:2] = jnp.where(hit, wide[1:2], stat_ref[2:3] / total)

    p = jnp.exp2(s - log_s) * times
    ds = (p * (dp - dot_s)).astype(BF16)
    dk = nn(ds, qs)
    dv = nn(p.astype(BF16), gs)
    dqf_ref[...] = tn(ds, kf[...])
    pf_ref[0] = dk[:FAR8]
    pf_ref[1] = dv[:FAR8]
    lo = FAR8
    for ref, size in ((h2_ref, FAR16), (h4_ref, FAR32), (h6_ref, FAR32)):
        for j in range(2):
            ref[j, 0] = dk[lo : lo + size].astype(BF16)
            ref[j, 1] = dv[lo : lo + size].astype(BF16)
            lo += size


def far_part(offsets, kv8, qg8, far, stat, some):
    out = [
        jax.ShapeDtypeStruct((8, ROW), F32),
        jax.ShapeDtypeStruct((2, 2, FAR16, HD), BF16),
        jax.ShapeDtypeStruct((2, 2, FAR32, HD), BF16),
        jax.ShapeDtypeStruct((2, 2, FAR32, HD), BF16),
        jax.ShapeDtypeStruct((FAR8, HD), F32),
        jax.ShapeDtypeStruct((2, FAR8, HD), F32),
    ]
    scratch = [
        pltpu.VMEM((FARK, HD), BF16),
        pltpu.VMEM((FARK, HD), BF16),
        pltpu.VMEM((8, FAR8), F32),
    ]
    return call(far_kernel, out, scratch, smem=(0,), nin=8)(
        offsets, kv8, qg8, *far, stat, some
    )


def back_prev_kernel(kv_ref, qg_ref, fin_ref, acc, dq_ref):
    plane, _ = place()
    there = plane > 0
    seen = iota((SLAB, SLAB), 0) > iota((SLAB, SLAB), 1)
    for kb in range(COLS):
        k = kv_ref[0, rows_of(kb)]
        v = kv_ref[1, rows_of(kb)]
        dk = jnp.zeros((SLAB, HD), F32)
        dv = jnp.zeros((SLAB, HD), F32)
        for qb in range(kb + 1):
            lanes = pl.ds(qb * SLAB, SLAB)
            q = qg_ref[0, rows_of(qb)]
            g = qg_ref[1, rows_of(qb)]
            log = jnp.where(there, fin_ref[0:1, lanes], -NEG)
            s = nt(k, q) * C2 - log
            if kb == qb:
                s = jnp.where(seen, s, NEG)
            p = jnp.exp2(s)
            ds = (p * (nt(v, g) - fin_ref[1:2, lanes])).astype(BF16)
            dv = dv + nn(p.astype(BF16), g)
            dk = dk + nn(ds, q)
            part = tn(k, ds)
            dq_ref[:, lanes] = part if kb == qb else dq_ref[:, lanes] + part
        acc[0, rows_of(kb)] = dk
        acc[1, rows_of(kb)] = dv


def back_prev(kv, qg, fin):
    out = [jax.ShapeDtypeStruct((2, ROW, HD), F32), jax.ShapeDtypeStruct((HD, ROW), F32)]
    return call(back_prev_kernel, out, nin=3)(kv, qg, fin)


def merge_kernel(off_ref, prev_ref, pf_ref, a2_ref, a4_ref, a6_ref, out_ref, acc):
    _, col = place()
    off = off_ref[col]
    every8th = pl.ds(off % 8, FAR8, stride=8)
    every16 = pl.ds(off % 16, FAR16, stride=16)
    every32 = pl.ds(off % 32, FAR32, stride=32)
    for which in range(2):
        acc[...] = prev_ref[which]
        acc[every8th, :] = acc[every8th, :] + pf_ref[which]
        acc[every16, :] = acc[every16, :] + a2_ref[1, which].astype(F32)
        acc[every32, :] = acc[every32, :] + (
            a4_ref[1, which].astype(F32) + a6_ref[1, which].astype(F32)
        )
        out_ref[which] = acc[...].astype(BF16)


def merge(offsets, prev, pf, a2, a4, a6):
    out = jax.ShapeDtypeStruct((2, ROW, HD), BF16)
    return call(merge_kernel, out, [pltpu.VMEM((ROW, HD), F32)], smem=(0,), nin=6)(
        offsets, prev, pf, a2, a4, a6
    )


def back_own_kernel(off_ref, kv_ref, qg_ref, fin_ref, tab_ref, dqp_ref, dqf_ref, *refs):
    dq_out = refs[:COLS]
    own_ref, dqt, dq = refs[COLS:]
    _, col = place()
    strided = pl.ds(off_ref[col] % 8, FAR8, stride=8)
    seen = iota((SLAB, SLAB), 0) <= iota((SLAB, SLAB), 1)
    for qb in range(COLS):
        lanes = pl.ds(qb * SLAB, SLAB)
        q = qg_ref[0, rows_of(qb)]
        g = qg_ref[1, rows_of(qb)]
        dq_sum = dqp_ref[:, lanes]
        for kb in range(qb + 1):
            k = kv_ref[0, rows_of(kb)]
            s = nt(k, q) * C2 - fin_ref[0:1, lanes]
            if kb == qb:
                s = jnp.where(seen, s, NEG)
            p = jnp.exp2(s) * tab_ref[int(kb // 2 == qb // 2)]
            ds = (p * (nt(kv_ref[1, rows_of(kb)], g) - fin_ref[1:2, lanes])).astype(BF16)
            dv = nn(p.astype(BF16), g)
            dk = nn(ds, q)
            dq_sum = dq_sum + tn(k, ds)
            if kb == qb:
                own_ref[0, rows_of(kb)] = dk
                own_ref[1, rows_of(kb)] = dv
            else:
                own_ref[0, rows_of(kb)] += dk
                own_ref[1, rows_of(kb)] += dv
        dq[rows_of(qb)] = dq_sum.T
    dq[strided, :] = dq[strided, :] + dqf_ref[...]
    for step in range(COLS):
        rows = pl.ds(pl.multiple_of(((col + step) % COLS) * SLAB, SLAB), SLAB)
        dq_out[step][...] = (dq[rows] * SCALE).astype(BF16)


def back_own(offsets, kv, qg, fin, tab, dqp, dqf):
    out = [jax.ShapeDtypeStruct((SLAB, HD), BF16)] * COLS + [
        jax.ShapeDtypeStruct((2, ROW, HD), F32)
    ]
    scratch = [pltpu.VMEM((HD, ROW), F32), pltpu.VMEM((ROW, HD), F32)]
    return call(back_own_kernel, out, scratch, smem=(0,), nin=7)(
        offsets, kv, qg, fin, tab, dqp, dqf
    )


def join_kernel(off_ref, own_ref, near_ref, a2_ref, a4_ref, a6_ref, *refs):
    out = refs[:COLS]
    acc = refs[COLS]
    _, col = place()
    off = off_ref[col]
    every16 = pl.ds(off % 16, FAR16, stride=16)
    every32 = pl.ds(off % 32, FAR32, stride=32)
    for which in range(2):
        acc[...] = own_ref[which] + near_ref[which].astype(F32)
        acc[every16, :] = acc[every16, :] + a2_ref[0, which].astype(F32)
        acc[every32, :] = acc[every32, :] + (
            a4_ref[0, which].astype(F32) + a6_ref[0, which].astype(F32)
        )
        for step in range(COLS):
            rows = pl.ds(pl.multiple_of(((col + step) % COLS) * SLAB, SLAB), SLAB)
            value = acc[rows]
            if which == 0:
                value = value * SCALE
            out[step][which] = value.astype(BF16)


def join(offsets, own, near, a2, a4, a6):
    piece = jax.ShapeDtypeStruct((2, SLAB, HD), BF16)
    return call(
        join_kernel, [piece] * COLS, [pltpu.VMEM((ROW, HD), F32)], smem=(0,), nin=6
    )(offsets, own, near, a2, a4, a6)


def spread_kernel(*refs):
    dq_in = refs[:COLS]
    kv_in = refs[COLS : 2 * COLS]
    q_ref, k_ref, v_ref = refs[2 * COLS :]
    _, col = place()
    for step in range(COLS):
        lanes = pl.ds(pl.multiple_of(((col - step + COLS) % COLS) * HD, HD), HD)
        q_ref[:, lanes] = dq_in[step][...]
        k_ref[:, lanes] = kv_in[step][0]
        v_ref[:, lanes] = kv_in[step][1]


def spread(dq, dkv):
    out = jax.ShapeDtypeStruct((SLAB, COLS * HD), BF16)
    return call(spread_kernel, [out] * 3, nin=2 * COLS)(*dq, *dkv)


def body(planes, query_states, key_states, value_states, out_grad, head_offsets):
    def exchange(pieces):
        return [pieces[0]] + [across(pieces[s], s, planes) for s in range(1, COLS)]

    kv = exchange(pack(key_states, value_states))
    qg = exchange(pack(query_states, out_grad))
    row = stack(kv)
    prev = along(row, 1, planes)
    stat_own, qg, tab, qg8 = first_own(head_offsets, row, qg)
    prev, stat_own = lax.optimization_barrier((prev, stat_own))
    wide, slim = pair_up(head_offsets, row, prev)
    far = [along(wide, 2, planes), along(slim, 4, planes), along(slim, 6, planes)]
    stat, some, kv8 = first_prev(head_offsets, prev, qg, stat_own)
    fin, h2, h4, h6, dqf, pf = far_part(head_offsets, kv8, qg8, far, stat, some)
    a2, a4, a6 = [along(h, -step, planes) for h, step in ((h2, 2), (h4, 4), (h6, 6))]
    prev_grad, dqp = back_prev(prev, qg, fin)
    results = back_own(head_offsets, row, qg, fin, tab, dqp, dqf)
    own, prev_grad = lax.optimization_barrier((results[COLS], prev_grad))
    near = along(merge(head_offsets, prev_grad, pf, a2, a4, a6), -1, planes)
    dq = exchange(results[:COLS])
    near, *dq = lax.optimization_barrier((near, *dq))
    dkv = exchange(join(head_offsets, own, near, a2, a4, a6))
    return tuple(spread(dq, dkv))


def solution(mesh):
    spec = P(("batch", "seq"), "head")
    planes = mesh.shape["seq"] // COLS
    return jax.shard_map(
        functools.partial(body, planes),
        mesh=mesh,
        in_specs=(spec, spec, spec, spec, P("head")),
        out_specs=(spec, spec, spec),
        check_vma=False,
    )
```

```python
import functools

import jax
import jax.numpy as jnp
from jax import lax
from jax.experimental import pallas as pl
from jax.experimental.pallas import tpu as pltpu
from jax.sharding import PartitionSpec as P

COLS = 4
SLAB = 256
HD = 128
ROW = COLS * SLAB
NEG = -1e30
SCALE = HD**-0.5
LOG2E = 1.4426950408889634
FAR8 = ROW // 8
FAR16 = ROW // 16
FAR32 = ROW // 32
THIN16 = SLAB // 16
THIN32 = SLAB // 32
FARK = FAR8 + 2 * FAR16 + 4 * FAR32
C2 = SCALE * LOG2E
F32 = jnp.float32
BF16 = jnp.bfloat16


def across(value, step, planes):
    pairs = [
        (p * COLS + c, p * COLS + (c + step) % COLS) for p in range(planes) for c in range(COLS)
    ]
    return lax.ppermute(value, "seq", pairs)


def along(value, step, planes):
    pairs = [
        (p * COLS + c, (p + step) % planes * COLS + c) for p in range(planes) for c in range(COLS)
    ]
    return lax.ppermute(value, "seq", pairs)


def place():
    pos = lax.axis_index("seq")
    return pos // COLS, pos % COLS


def mm(left, right, dims):
    return lax.dot_general(left, right, (dims, ((), ())), preferred_element_type=F32)


def nn(left, right):
    return mm(left, right, ((1,), (0,)))


def nt(left, right):
    return mm(left, right, ((1,), (1,)))


def tn(left, right):
    return mm(left, right, ((0,), (0,)))


def call(kernel, out, scratch=(), smem=(), nin=0):
    here = pltpu.VMEM
    specs = [pl.BlockSpec(memory_space=pltpu.SMEM if i in smem else here) for i in range(nin)]
    return pl.pallas_call(
        kernel,
        out_shape=out,
        in_specs=specs,
        out_specs=jax.tree.map(lambda _: pl.BlockSpec(memory_space=here), out),
        scratch_shapes=scratch,
        compiler_params=pltpu.CompilerParams(vmem_limit_bytes=24 << 20),
        cost_estimate=pl.CostEstimate(flops=1, bytes_accessed=1, transcendentals=0),
    )


def pack_kernel(one_ref, two_ref, *out_refs):
    _, col = place()
    for step in range(COLS):
        lanes = pl.ds(pl.multiple_of(((col + step) % COLS) * HD, HD), HD)
        out_refs[step][0] = one_ref[:, lanes]
        out_refs[step][1] = two_ref[:, lanes]


def pack(one, two):
    piece = jax.ShapeDtypeStruct((2, SLAB, HD), BF16)
    return call(pack_kernel, [piece] * COLS, nin=2)(one, two)


def pick(stride, rest, rows, width):
    r = lax.broadcasted_iota(jnp.int32, (rows, width), 0)
    c = lax.broadcasted_iota(jnp.int32, (rows, width), 1)
    return (c == r * stride + rest).astype(BF16)


def rows_of(block):
    return pl.ds(block * SLAB, SLAB)


def stack_kernel(*refs):
    out_ref = refs[COLS - 1]
    for i in range(COLS - 1):
        for which in range(2):
            out_ref[which, rows_of(i)] = refs[i][which]


def stack(pieces):
    out = jax.ShapeDtypeStruct((2, ROW - SLAB, HD), BF16)
    return call(stack_kernel, out, nin=COLS - 1)(*pieces)


def place_rows(out_ref, col, step, which, value):
    slab = (col - step + COLS) % COLS
    out_ref[which, pl.ds(pl.multiple_of(slab * SLAB, SLAB), SLAB)] = value


def pair_kernel(off_ref, *refs):
    mine = refs[:COLS]
    first_ref, rest_ref, prev_ref, wide_ref, slim_ref = refs[COLS:]
    _, col = place()
    off = off_ref[col]
    by16 = pick(16, off % 16, THIN16, SLAB)
    by32 = pick(32, off % 32, THIN32, SLAB)
    for step in range(COLS):
        slab = (col - step + COLS) % COLS
        few = pl.ds(pl.multiple_of(slab * THIN16, THIN16), THIN16)
        less = pl.ds(pl.multiple_of(slab * THIN32, THIN32), THIN32)
        for which in range(2):
            back = first_ref[which] if step == 0 else rest_ref[which, rows_of(step - 1)]
            place_rows(prev_ref, col, step, which, back)
            for j, value in enumerate((mine[step][which], back)):
                wide_ref[j, which, few] = nn(by16, value).astype(BF16)
                slim_ref[j, which, less] = nn(by32, value).astype(BF16)


def pair_up(offsets, mine, first, rest):
    out = [
        jax.ShapeDtypeStruct((2, ROW, HD), BF16),
        jax.ShapeDtypeStruct((2, 2, FAR16, HD), BF16),
        jax.ShapeDtypeStruct((2, 2, FAR32, HD), BF16),
    ]
    return call(pair_kernel, out, smem=(0,), nin=3 + COLS)(offsets, *mine, first, rest)


def depth_of(index, off):
    rest = (index - off) & 31
    total = jnp.zeros(index.shape, F32)
    for level in range(1, 6):
        total = total + ((rest & (2**level - 1)) == 0).astype(F32)
    return total


def iota(shape, axis):
    return lax.broadcasted_iota(jnp.int32, shape, axis)


def thinned(thin8, from_ref, few_ref):
    for which in range(2):
        for b in range(COLS):
            rows = pl.ds(b * (SLAB // 8), SLAB // 8)
            few_ref[which, rows] = nn(thin8, from_ref[which, rows_of(b)]).astype(BF16)


def first_own_kernel(off_ref, *refs):
    kv = refs[:COLS]
    qg = refs[COLS : 2 * COLS]
    stat_ref, kv_ref, qg_ref, tab_ref, few_ref, sc = refs[2 * COLS :]
    _, col = place()
    off = off_ref[col]
    thin8 = pick(8, off % 8, SLAB // 8, SLAB)
    for step in range(COLS):
        for which in range(2):
            place_rows(kv_ref, col, step, which, kv[step][which])
            place_rows(qg_ref, col, step, which, qg[step][which])
    thinned(thin8, qg_ref, few_ref)
    deep_k = depth_of(iota((SLAB, HD), 0), off)
    deep_k = jnp.concatenate([deep_k, deep_k], axis=1)
    deep_q = depth_of(iota((8, SLAB), 1), off)[:1]
    both = jnp.minimum(deep_k, deep_q)
    tab_ref[0] = 1.0 + jnp.maximum(both - 1.0, 0.0)
    tab_ref[1] = 1.0 + both
    stat_ref[...] = jnp.zeros((8, ROW), F32)
    seen = iota((SLAB, SLAB), 0) <= iota((SLAB, SLAB), 1)
    for qb in range(COLS):
        q = qg_ref[0, rows_of(qb)]
        g = qg_ref[1, rows_of(qb)]
        m = None
        for kb in range(qb + 1):
            s = nt(kv_ref[0, rows_of(kb)], q) * C2
            if kb == qb:
                s = jnp.where(seen, s, NEG)
            sc[rows_of(kb)] = s
            top = jnp.max(s, axis=0, keepdims=True)
            m = top if m is None else jnp.maximum(m, top)
        total = jnp.zeros((1, SLAB), F32)
        dot = jnp.zeros((1, SLAB), F32)
        for kb in range(qb + 1):
            e = jnp.exp2(sc[rows_of(kb)] - m)
            dp = nt(kv_ref[1, rows_of(kb)], g) * tab_ref[int(kb // 2 == qb // 2)]
            total = total + jnp.sum(
                e * tab_ref[int(kb // 2 == qb // 2)], axis=0, keepdims=True
            )
            dot = dot + jnp.sum(e.astype(BF16).astype(F32) * dp, axis=0, keepdims=True)
        lanes = pl.ds(qb * SLAB, SLAB)
        stat_ref[0:1, lanes] = m
        stat_ref[1:2, lanes] = total
        stat_ref[2:3, lanes] = dot


def first_own(offsets, kv, qg):
    out = [
        jax.ShapeDtypeStruct((8, ROW), F32),
        jax.ShapeDtypeStruct((2, ROW, HD), BF16),
        jax.ShapeDtypeStruct((2, ROW, HD), BF16),
        jax.ShapeDtypeStruct((2, SLAB, SLAB), F32),
        jax.ShapeDtypeStruct((2, FAR8, HD), BF16),
    ]
    scratch = [pltpu.VMEM((ROW, SLAB), F32)]
    return call(first_own_kernel, out, scratch, smem=(0,), nin=1 + 2 * COLS)(
        offsets, *kv, *qg
    )


def first_prev_kernel(
    off_ref, kv_ref, qg_ref, so_ref, stat_ref, some_ref, few_ref, sc
):
    plane, col = place()
    rest8 = off_ref[col] % 8
    thinned(pick(8, rest8, SLAB // 8, SLAB), kv_ref, few_ref)
    there = plane > 0
    stat_ref[...] = jnp.zeros((8, ROW), F32)
    seen = iota((SLAB, SLAB), 0) > iota((SLAB, SLAB), 1)
    for qb in range(COLS):
        q = qg_ref[0, rows_of(qb)]
        g = qg_ref[1, rows_of(qb)]
        m = None
        for kb in range(qb, COLS):
            s = nt(kv_ref[0, rows_of(kb)], q) * C2
            if kb == qb:
                s = jnp.where(seen, s, NEG)
            sc[rows_of(kb)] = s
            top = jnp.max(s, axis=0, keepdims=True)
            m = top if m is None else jnp.maximum(m, top)
        total = jnp.zeros((1, SLAB), F32)
        dot = jnp.zeros((1, SLAB), F32)
        for kb in range(qb, COLS):
            s = sc[rows_of(kb)]
            e = jnp.exp2(s - m)
            if kb == qb:
                e = jnp.where(seen, e, 0.0)
            total = total + jnp.sum(e, axis=0, keepdims=True)
            dp = nt(kv_ref[1, rows_of(kb)], g)
            dot = dot + jnp.sum(e.astype(BF16).astype(F32) * dp, axis=0, keepdims=True)
        lanes = pl.ds(qb * SLAB, SLAB)
        mp = jnp.where(there, m, NEG)
        mo = so_ref[0:1, lanes]
        m = jnp.maximum(mo, mp)
        fo = jnp.exp2(mo - m)
        fp = jnp.where(there, jnp.exp2(mp - m), 0.0)
        stat_ref[0:1, lanes] = m
        stat_ref[1:2, lanes] = so_ref[1:2, lanes] * fo + total * fp
        stat_ref[2:3, lanes] = so_ref[2:3, lanes] * fo + dot * fp
    some_ref[...] = moved(stat_ref[...], every8(rest8), ((1,), (1,)))


def every8(rest8):
    return (iota((FAR8, ROW), 1) == iota((FAR8, ROW), 0) * 8 + rest8).astype(BF16)


def moved(values, chosen, dims):
    high = values.astype(BF16)
    rest = values - high.astype(F32)
    mid = rest.astype(BF16)
    low = (rest - mid.astype(F32)).astype(BF16)
    return mm(high, chosen, dims) + mm(mid, chosen, dims) + mm(low, chosen, dims)


def first_prev(offsets, kv, qg, stat_own):
    out = [
        jax.ShapeDtypeStruct((8, ROW), F32),
        jax.ShapeDtypeStruct((8, FAR8), F32),
        jax.ShapeDtypeStruct((2, FAR8, HD), BF16),
    ]
    scratch = [pltpu.VMEM((ROW, SLAB), F32)]
    return call(first_prev_kernel, out, scratch, smem=(0,), nin=4)(
        offsets, kv, qg, stat_own
    )


def far_kernel(
    off_ref, kv8_ref, qg8_ref, g2_ref, g4_ref, g6_ref, stat_ref, some_ref,
    fin_ref, h2_ref, h4_ref, h6_ref, dqf_ref, pf_ref, kf, vf, near,
):
    plane, col = place()
    off = off_ref[col]
    rest8 = off % 8
    kf[pl.ds(0, FAR8)] = kv8_ref[0]
    vf[pl.ds(0, FAR8)] = kv8_ref[1]
    lo = FAR8
    for ref, size in ((g2_ref, FAR16), (g4_ref, FAR32), (g6_ref, FAR32)):
        for j in range(2):
            kf[pl.ds(lo, size)] = ref[j, 0]
            vf[pl.ds(lo, size)] = ref[j, 1]
            lo += size
    qs = qg8_ref[0]
    gs = qg8_ref[1]
    r = iota((FARK, HD), 0)
    mid = r - FAR8
    end = mid - 2 * FAR16
    back = jnp.where(r < FAR8, 1, jnp.where(end < 0, 2 + mid // FAR16, 4 + end // FAR32))
    spot = jnp.where(
        r < FAR8,
        r * 8 + rest8,
        jnp.where(end < 0, (mid % FAR16) * 16 + off % 16, (end % FAR32) * 32 + off % 32),
    )
    other = plane - back
    first = jnp.where(
        other < 0,
        9,
        jnp.where(other // 2 == plane // 2, 3, jnp.where(other // 4 == plane // 4, 4, 5)),
    )
    deep_q = depth_of(iota((8, FAR8), 1) * 8 + rest8, off)[:1]
    deep = jnp.minimum(deep_q, depth_of(spot, off))
    times = jnp.maximum(deep - first.astype(F32) + 1.0, 0.0)
    s = jnp.where(times > 0.0, nt(kf[...], qs) * C2, NEG)
    dp = nt(vf[...], gs)
    m_f = jnp.max(s, axis=0, keepdims=True)
    e = jnp.exp2(s - m_f)
    l_f = jnp.sum(e * times, axis=0, keepdims=True)
    d_f = jnp.sum(e.astype(BF16).astype(F32) * (dp * times), axis=0, keepdims=True)

    m_n, l_n, d_n = some_ref[0:1], some_ref[1:2], some_ref[2:3]
    m_s = jnp.maximum(m_n, m_f)
    fn = jnp.exp2(m_n - m_s)
    ff = jnp.exp2(m_f - m_s)
    l_s = l_n * fn + l_f * ff
    log_s = m_s + jnp.log2(l_s)
    dot_s = (d_n * fn + d_f * ff) / l_s
    near[...] = jnp.zeros((8, FAR8), F32)
    near[0:1] = log_s
    near[1:2] = dot_s
    wide = moved(near[...], every8(rest8), ((1,), (0,)))
    hit = (iota((8, ROW), 1) % 8 == rest8)[:1]
    fin_ref[...] = jnp.zeros((8, ROW), F32)
    total = stat_ref[1:2]
    fin_ref[0:1] = jnp.where(hit, wide[0:1], stat_ref[0:1] + jnp.log2(total))
    fin_ref[1:2] = jnp.where(hit, wide[1:2], stat_ref[2:3] / total)

    p = jnp.exp2(s - log_s) * times
    ds = (p * (dp - dot_s)).astype(BF16)
    dk = nn(ds, qs)
    dv = nn(p.astype(BF16), gs)
    dqf_ref[...] = tn(ds, kf[...])
    pf_ref[0] = dk[:FAR8]
    pf_ref[1] = dv[:FAR8]
    lo = FAR8
    for ref, size in ((h2_ref, FAR16), (h4_ref, FAR32), (h6_ref, FAR32)):
        for j in range(2):
            ref[j, 0] = dk[lo : lo + size].astype(BF16)
            ref[j, 1] = dv[lo : lo + size].astype(BF16)
            lo += size


def far_part(offsets, kv8, qg8, far, stat, some):
    out = [
        jax.ShapeDtypeStruct((8, ROW), F32),
        jax.ShapeDtypeStruct((2, 2, FAR16, HD), BF16),
        jax.ShapeDtypeStruct((2, 2, FAR32, HD), BF16),
        jax.ShapeDtypeStruct((2, 2, FAR32, HD), BF16),
        jax.ShapeDtypeStruct((FAR8, HD), F32),
        jax.ShapeDtypeStruct((2, FAR8, HD), F32),
    ]
    scratch = [
        pltpu.VMEM((FARK, HD), BF16),
        pltpu.VMEM((FARK, HD), BF16),
        pltpu.VMEM((8, FAR8), F32),
    ]
    return call(far_kernel, out, scratch, smem=(0,), nin=8)(
        offsets, kv8, qg8, *far, stat, some
    )


def back_prev_kernel(kv_ref, qg_ref, fin_ref, acc, dq_ref):
    plane, _ = place()
    there = plane > 0
    seen = iota((SLAB, SLAB), 0) > iota((SLAB, SLAB), 1)
    for kb in range(COLS):
        k = kv_ref[0, rows_of(kb)]
        v = kv_ref[1, rows_of(kb)]
        dk = jnp.zeros((SLAB, HD), F32)
        dv = jnp.zeros((SLAB, HD), F32)
        for qb in range(kb + 1):
            lanes = pl.ds(qb * SLAB, SLAB)
            q = qg_ref[0, rows_of(qb)]
            g = qg_ref[1, rows_of(qb)]
            log = jnp.where(there, fin_ref[0:1, lanes], -NEG)
            s = nt(k, q) * C2 - log
            if kb == qb:
                s = jnp.where(seen, s, NEG)
            p = jnp.exp2(s)
            ds = (p * (nt(v, g) - fin_ref[1:2, lanes])).astype(BF16)
            dv = dv + nn(p.astype(BF16), g)
            dk = dk + nn(ds, q)
            part = tn(k, ds)
            dq_ref[:, lanes] = part if kb == qb else dq_ref[:, lanes] + part
        acc[0, rows_of(kb)] = dk
        acc[1, rows_of(kb)] = dv


def back_prev(kv, qg, fin):
    out = [jax.ShapeDtypeStruct((2, ROW, HD), F32), jax.ShapeDtypeStruct((HD, ROW), F32)]
    return call(back_prev_kernel, out, nin=3)(kv, qg, fin)


def merge_kernel(off_ref, prev_ref, pf_ref, a2_ref, a4_ref, a6_ref, out_ref, acc):
    _, col = place()
    off = off_ref[col]
    every8th = pl.ds(off % 8, FAR8, stride=8)
    every16 = pl.ds(off % 16, FAR16, stride=16)
    every32 = pl.ds(off % 32, FAR32, stride=32)
    for which in range(2):
        acc[...] = prev_ref[which]
        acc[every8th, :] = acc[every8th, :] + pf_ref[which]
        acc[every16, :] = acc[every16, :] + a2_ref[1, which].astype(F32)
        acc[every32, :] = acc[every32, :] + (
            a4_ref[1, which].astype(F32) + a6_ref[1, which].astype(F32)
        )
        out_ref[which] = acc[...].astype(BF16)


def merge(offsets, prev, pf, a2, a4, a6):
    out = jax.ShapeDtypeStruct((2, ROW, HD), BF16)
    return call(merge_kernel, out, [pltpu.VMEM((ROW, HD), F32)], smem=(0,), nin=6)(
        offsets, prev, pf, a2, a4, a6
    )


def back_own_kernel(off_ref, kv_ref, qg_ref, fin_ref, tab_ref, dqp_ref, dqf_ref, *refs):
    own_ref, dq_ref, dq = refs
    _, col = place()
    strided = pl.ds(off_ref[col] % 8, FAR8, stride=8)
    seen = iota((SLAB, SLAB), 0) <= iota((SLAB, SLAB), 1)
    for qb in range(COLS):
        lanes = pl.ds(qb * SLAB, SLAB)
        q = qg_ref[0, rows_of(qb)]
        g = qg_ref[1, rows_of(qb)]
        dq_sum = dqp_ref[:, lanes]
        for kb in range(qb + 1):
            k = kv_ref[0, rows_of(kb)]
            s = nt(k, q) * C2 - fin_ref[0:1, lanes]
            if kb == qb:
                s = jnp.where(seen, s, NEG)
            p = jnp.exp2(s) * tab_ref[int(kb // 2 == qb // 2)]
            ds = (p * (nt(kv_ref[1, rows_of(kb)], g) - fin_ref[1:2, lanes])).astype(BF16)
            dv = nn(p.astype(BF16), g)
            dk = nn(ds, q)
            dq_sum = dq_sum + tn(k, ds)
            if kb == qb:
                own_ref[0, rows_of(kb)] = dk
                own_ref[1, rows_of(kb)] = dv
            else:
                own_ref[0, rows_of(kb)] += dk
                own_ref[1, rows_of(kb)] += dv
        dq[rows_of(qb)] = dq_sum.T
    dq[strided, :] = dq[strided, :] + dqf_ref[...]
    dq_ref[...] = (dq[...] * SCALE).astype(BF16)


def back_own(offsets, kv, qg, fin, tab, dqp, dqf):
    out = [jax.ShapeDtypeStruct((2, ROW, HD), F32), jax.ShapeDtypeStruct((ROW, HD), BF16)]
    scratch = [pltpu.VMEM((ROW, HD), F32)]
    return call(back_own_kernel, out, scratch, smem=(0,), nin=7)(
        offsets, kv, qg, fin, tab, dqp, dqf
    )


def join_kernel(off_ref, dq_ref, own_ref, near_ref, a2_ref, a4_ref, a6_ref, *refs):
    out = refs[:COLS]
    acc = refs[COLS]
    _, col = place()
    off = off_ref[col]
    every16 = pl.ds(off % 16, FAR16, stride=16)
    every32 = pl.ds(off % 32, FAR32, stride=32)
    for which in range(2):
        acc[...] = own_ref[which] + near_ref[which].astype(F32)
        acc[every16, :] = acc[every16, :] + a2_ref[0, which].astype(F32)
        acc[every32, :] = acc[every32, :] + (
            a4_ref[0, which].astype(F32) + a6_ref[0, which].astype(F32)
        )
        for step in range(COLS):
            rows = pl.ds(pl.multiple_of(((col + step) % COLS) * SLAB, SLAB), SLAB)
            value = acc[rows]
            if which == 0:
                value = value * SCALE
                out[step][2] = dq_ref[rows]
            out[step][which] = value.astype(BF16)


def join(offsets, dq, own, near, a2, a4, a6):
    piece = jax.ShapeDtypeStruct((3, SLAB, HD), BF16)
    return call(
        join_kernel, [piece] * COLS, [pltpu.VMEM((ROW, HD), F32)], smem=(0,), nin=7
    )(offsets, dq, own, near, a2, a4, a6)


def spread_kernel(*refs):
    q_ref, k_ref, v_ref = refs[COLS:]
    _, col = place()
    for step in range(COLS):
        lanes = pl.ds(pl.multiple_of(((col - step + COLS) % COLS) * HD, HD), HD)
        q_ref[:, lanes] = refs[step][2]
        k_ref[:, lanes] = refs[step][0]
        v_ref[:, lanes] = refs[step][1]


def spread(pieces):
    out = jax.ShapeDtypeStruct((SLAB, COLS * HD), BF16)
    return call(spread_kernel, [out] * 3, nin=COLS)(*pieces)


def body(planes, query_states, key_states, value_states, out_grad, head_offsets):
    def exchange(pieces):
        return [pieces[0]] + [across(pieces[s], s, planes) for s in range(1, COLS)]

    kv = exchange(pack(key_states, value_states))
    qg = exchange(pack(query_states, out_grad))
    first = along(kv[0], 1, planes)
    first, *rest = lax.optimization_barrier((first, *kv[1:]))
    rest = along(stack(rest), 1, planes)
    prev, wide, slim = pair_up(head_offsets, kv, first, rest)
    prev, qg[0] = lax.optimization_barrier((prev, qg[0]))
    stat_own, row, qg, tab, qg8 = first_own(head_offsets, kv, qg)
    far = [along(wide, 2, planes), along(slim, 4, planes), along(slim, 6, planes)]
    stat, some, kv8 = first_prev(head_offsets, prev, qg, stat_own)
    fin, h2, h4, h6, dqf, pf = far_part(head_offsets, kv8, qg8, far, stat, some)
    a2, a4, a6 = [along(h, -step, planes) for h, step in ((h2, 2), (h4, 4), (h6, 6))]
    prev_grad, dqp = back_prev(prev, qg, fin)
    near = along(merge(head_offsets, prev_grad, pf, a2, a4, a6), -1, planes)
    own, dq = back_own(head_offsets, row, qg, fin, tab, dqp, dqf)
    pieces = exchange(join(head_offsets, dq, own, near, a2, a4, a6))
    return tuple(spread(pieces))


def solution(mesh):
    spec = P(("batch", "seq"), "head")
    planes = mesh.shape["seq"] // COLS
    return jax.shard_map(
        functools.partial(body, planes),
        mesh=mesh,
        in_specs=(spec, spec, spec, spec, P("head")),
        out_specs=(spec, spec, spec),
        check_vma=False,
    )
```

```python
import functools

import jax
import jax.numpy as jnp
from jax import lax
from jax.experimental import pallas as pl
from jax.experimental.pallas import tpu as pltpu
from jax.sharding import PartitionSpec as P

COLS = 4
SLAB = 256
HD = 128
ROW = COLS * SLAB
NEG = -1e30
SCALE = HD**-0.5
LOG2E = 1.4426950408889634
FAR8 = ROW // 8
FAR16 = ROW // 16
FAR32 = ROW // 32
THIN16 = SLAB // 16
THIN32 = SLAB // 32
FARK = FAR8 + 2 * FAR16 + 4 * FAR32
C2 = SCALE * LOG2E
F32 = jnp.float32
BF16 = jnp.bfloat16


ORDER = (0, 2, 1, 3)


def across(value, step, planes):
    pairs = [
        (p * COLS + c, p * COLS + (c + step) % COLS) for p in range(planes) for c in range(COLS)
    ]
    return lax.ppermute(value, "seq", pairs)


def along(value, step, planes):
    pairs = [
        (p * COLS + c, (p + step) % planes * COLS + c) for p in range(planes) for c in range(COLS)
    ]
    return lax.ppermute(value, "seq", pairs)


def place():
    pos = lax.axis_index("seq")
    return pos // COLS, pos % COLS


def mm(left, right, dims):
    return lax.dot_general(left, right, (dims, ((), ())), preferred_element_type=F32)


def nn(left, right):
    return mm(left, right, ((1,), (0,)))


def nt(left, right):
    return mm(left, right, ((1,), (1,)))


def tn(left, right):
    return mm(left, right, ((0,), (0,)))


def call(kernel, out, scratch=(), smem=(), nin=0):
    here = pltpu.VMEM
    specs = [pl.BlockSpec(memory_space=pltpu.SMEM if i in smem else here) for i in range(nin)]
    return pl.pallas_call(
        kernel,
        out_shape=out,
        in_specs=specs,
        out_specs=jax.tree.map(lambda _: pl.BlockSpec(memory_space=here), out),
        scratch_shapes=scratch,
        compiler_params=pltpu.CompilerParams(vmem_limit_bytes=24 << 20),
        cost_estimate=pl.CostEstimate(flops=1, bytes_accessed=1, transcendentals=0),
    )


def pack_kernel(one_ref, two_ref, *out_refs):
    _, col = place()
    for step in range(COLS):
        lanes = pl.ds(pl.multiple_of(((col + step) % COLS) * HD, HD), HD)
        out_refs[step][0] = one_ref[:, lanes]
        out_refs[step][1] = two_ref[:, lanes]


def pack(one, two):
    piece = jax.ShapeDtypeStruct((2, SLAB, HD), BF16)
    return call(pack_kernel, [piece] * COLS, nin=2)(one, two)


def pick(stride, rest, rows, width):
    r = lax.broadcasted_iota(jnp.int32, (rows, width), 0)
    c = lax.broadcasted_iota(jnp.int32, (rows, width), 1)
    return (c == r * stride + rest).astype(BF16)


def rows_of(block):
    return pl.ds(block * SLAB, SLAB)


def stack_kernel(*refs):
    out_ref = refs[COLS - 1]
    for i in range(COLS - 1):
        for which in range(2):
            out_ref[which, rows_of(i)] = refs[i][which]


def stack(pieces):
    out = jax.ShapeDtypeStruct((2, ROW - SLAB, HD), BF16)
    return call(stack_kernel, out, nin=COLS - 1)(*pieces)


def place_rows(out_ref, col, step, which, value):
    slab = (col - step + COLS) % COLS
    out_ref[which, pl.ds(pl.multiple_of(slab * SLAB, SLAB), SLAB)] = value


def prep_kernel(off_ref, *refs):
    mine = refs[:COLS]
    row_ref, wide_ref, slim_ref, tab_ref = refs[COLS:]
    _, col = place()
    off = off_ref[col]
    by16 = pick(16, off % 16, THIN16, SLAB)
    by32 = pick(32, off % 32, THIN32, SLAB)
    for step in range(COLS):
        slab = (col - step + COLS) % COLS
        few = pl.ds(pl.multiple_of(slab * THIN16, THIN16), THIN16)
        less = pl.ds(pl.multiple_of(slab * THIN32, THIN32), THIN32)
        for which in range(2):
            value = mine[step][which]
            place_rows(row_ref, col, step, which, value)
            wide_ref[which, few] = nn(by16, value).astype(BF16)
            slim_ref[which, less] = nn(by32, value).astype(BF16)
    deep_k = depth_of(iota((SLAB, HD), 0), off)
    deep_k = jnp.concatenate([deep_k, deep_k], axis=1)
    deep_q = depth_of(iota((8, SLAB), 1), off)[:1]
    both = jnp.minimum(deep_k, deep_q)
    tab_ref[0] = 1.0 + jnp.maximum(both - 1.0, 0.0)
    tab_ref[1] = 1.0 + both


def prepare(offsets, mine):
    out = [
        jax.ShapeDtypeStruct((2, ROW, HD), BF16),
        jax.ShapeDtypeStruct((2, FAR16, HD), BF16),
        jax.ShapeDtypeStruct((2, FAR32, HD), BF16),
        jax.ShapeDtypeStruct((2, SLAB, SLAB), F32),
    ]
    return call(prep_kernel, out, smem=(0,), nin=1 + COLS)(offsets, *mine)


def pair_kernel(off_ref, mw_ref, ms_ref, first_ref, rest_ref, prev_ref, wide_ref, slim_ref):
    _, col = place()
    off = off_ref[col]
    by16 = pick(16, off % 16, THIN16, SLAB)
    by32 = pick(32, off % 32, THIN32, SLAB)
    wide_ref[0] = mw_ref[...]
    slim_ref[0] = ms_ref[...]
    for step in range(COLS):
        slab = (col - step + COLS) % COLS
        few = pl.ds(pl.multiple_of(slab * THIN16, THIN16), THIN16)
        less = pl.ds(pl.multiple_of(slab * THIN32, THIN32), THIN32)
        for which in range(2):
            back = first_ref[which]
            if step > 0:
                back = rest_ref[which, rows_of(ORDER.index(step) - 1)]
            place_rows(prev_ref, col, step, which, back)
            wide_ref[1, which, few] = nn(by16, back).astype(BF16)
            slim_ref[1, which, less] = nn(by32, back).astype(BF16)


def pair_up(offsets, mine_wide, mine_slim, first, rest):
    out = [
        jax.ShapeDtypeStruct((2, ROW, HD), BF16),
        jax.ShapeDtypeStruct((2, 2, FAR16, HD), BF16),
        jax.ShapeDtypeStruct((2, 2, FAR32, HD), BF16),
    ]
    return call(pair_kernel, out, smem=(0,), nin=5)(offsets, mine_wide, mine_slim, first, rest)


def depth_of(index, off):
    rest = (index - off) & 31
    total = jnp.zeros(index.shape, F32)
    for level in range(1, 6):
        total = total + ((rest & (2**level - 1)) == 0).astype(F32)
    return total


def iota(shape, axis):
    return lax.broadcasted_iota(jnp.int32, shape, axis)


def thinned(thin8, from_ref, few_ref):
    for which in range(2):
        for b in range(COLS):
            rows = pl.ds(b * (SLAB // 8), SLAB // 8)
            few_ref[which, rows] = nn(thin8, from_ref[which, rows_of(b)]).astype(BF16)


def first_own_kernel(off_ref, kv_ref, tab_ref, *refs):
    qg = refs[:COLS]
    stat_ref, qg_ref, few_ref, sc = refs[COLS:]
    _, col = place()
    off = off_ref[col]
    thin8 = pick(8, off % 8, SLAB // 8, SLAB)
    for step in range(COLS):
        for which in range(2):
            place_rows(qg_ref, col, step, which, qg[step][which])
    thinned(thin8, qg_ref, few_ref)
    stat_ref[...] = jnp.zeros((8, ROW), F32)
    seen = iota((SLAB, SLAB), 0) <= iota((SLAB, SLAB), 1)
    for qb in range(COLS):
        q = qg_ref[0, rows_of(qb)]
        g = qg_ref[1, rows_of(qb)]
        m = None
        for kb in range(qb + 1):
            s = nt(kv_ref[0, rows_of(kb)], q) * C2
            if kb == qb:
                s = jnp.where(seen, s, NEG)
            sc[rows_of(kb)] = s
            top = jnp.max(s, axis=0, keepdims=True)
            m = top if m is None else jnp.maximum(m, top)
        total = jnp.zeros((1, SLAB), F32)
        dot = jnp.zeros((1, SLAB), F32)
        for kb in range(qb + 1):
            e = jnp.exp2(sc[rows_of(kb)] - m)
            dp = nt(kv_ref[1, rows_of(kb)], g) * tab_ref[int(kb // 2 == qb // 2)]
            total = total + jnp.sum(
                e * tab_ref[int(kb // 2 == qb // 2)], axis=0, keepdims=True
            )
            dot = dot + jnp.sum(e.astype(BF16).astype(F32) * dp, axis=0, keepdims=True)
        lanes = pl.ds(qb * SLAB, SLAB)
        stat_ref[0:1, lanes] = m
        stat_ref[1:2, lanes] = total
        stat_ref[2:3, lanes] = dot


def first_own(offsets, kv, tab, qg):
    out = [
        jax.ShapeDtypeStruct((8, ROW), F32),
        jax.ShapeDtypeStruct((2, ROW, HD), BF16),
        jax.ShapeDtypeStruct((2, FAR8, HD), BF16),
    ]
    scratch = [pltpu.VMEM((ROW, SLAB), F32)]
    return call(first_own_kernel, out, scratch, smem=(0,), nin=3 + COLS)(offsets, kv, tab, *qg)


def first_prev_kernel(
    off_ref, kv_ref, qg_ref, so_ref, stat_ref, some_ref, few_ref, sc
):
    plane, col = place()
    rest8 = off_ref[col] % 8
    thinned(pick(8, rest8, SLAB // 8, SLAB), kv_ref, few_ref)
    there = plane > 0
    stat_ref[...] = jnp.zeros((8, ROW), F32)
    seen = iota((SLAB, SLAB), 0) > iota((SLAB, SLAB), 1)
    for qb in range(COLS):
        q = qg_ref[0, rows_of(qb)]
        g = qg_ref[1, rows_of(qb)]
        m = None
        for kb in range(qb, COLS):
            s = nt(kv_ref[0, rows_of(kb)], q) * C2
            if kb == qb:
                s = jnp.where(seen, s, NEG)
            sc[rows_of(kb)] = s
            top = jnp.max(s, axis=0, keepdims=True)
            m = top if m is None else jnp.maximum(m, top)
        total = jnp.zeros((1, SLAB), F32)
        dot = jnp.zeros((1, SLAB), F32)
        for kb in range(qb, COLS):
            s = sc[rows_of(kb)]
            e = jnp.exp2(s - m)
            if kb == qb:
                e = jnp.where(seen, e, 0.0)
            total = total + jnp.sum(e, axis=0, keepdims=True)
            dp = nt(kv_ref[1, rows_of(kb)], g)
            dot = dot + jnp.sum(e.astype(BF16).astype(F32) * dp, axis=0, keepdims=True)
        lanes = pl.ds(qb * SLAB, SLAB)
        mp = jnp.where(there, m, NEG)
        mo = so_ref[0:1, lanes]
        m = jnp.maximum(mo, mp)
        fo = jnp.exp2(mo - m)
        fp = jnp.where(there, jnp.exp2(mp - m), 0.0)
        stat_ref[0:1, lanes] = m
        stat_ref[1:2, lanes] = so_ref[1:2, lanes] * fo + total * fp
        stat_ref[2:3, lanes] = so_ref[2:3, lanes] * fo + dot * fp
    some_ref[...] = moved(stat_ref[...], every8(rest8), ((1,), (1,)))


def every8(rest8):
    return (iota((FAR8, ROW), 1) == iota((FAR8, ROW), 0) * 8 + rest8).astype(BF16)


def moved(values, chosen, dims):
    high = values.astype(BF16)
    rest = values - high.astype(F32)
    mid = rest.astype(BF16)
    low = (rest - mid.astype(F32)).astype(BF16)
    return mm(high, chosen, dims) + mm(mid, chosen, dims) + mm(low, chosen, dims)


def first_prev(offsets, kv, qg, stat_own):
    out = [
        jax.ShapeDtypeStruct((8, ROW), F32),
        jax.ShapeDtypeStruct((8, FAR8), F32),
        jax.ShapeDtypeStruct((2, FAR8, HD), BF16),
    ]
    scratch = [pltpu.VMEM((ROW, SLAB), F32)]
    return call(first_prev_kernel, out, scratch, smem=(0,), nin=4)(
        offsets, kv, qg, stat_own
    )


def far_kernel(
    off_ref, kv8_ref, qg8_ref, g2_ref, g4_ref, g6_ref, stat_ref, some_ref,
    fin_ref, h2_ref, h4_ref, h6_ref, dqf_ref, pf_ref, kf, vf, near,
):
    plane, col = place()
    off = off_ref[col]
    rest8 = off % 8
    kf[pl.ds(0, FAR8)] = kv8_ref[0]
    vf[pl.ds(0, FAR8)] = kv8_ref[1]
    lo = FAR8
    for ref, size in ((g2_ref, FAR16), (g4_ref, FAR32), (g6_ref, FAR32)):
        for j in range(2):
            kf[pl.ds(lo, size)] = ref[j, 0]
            vf[pl.ds(lo, size)] = ref[j, 1]
            lo += size
    qs = qg8_ref[0]
    gs = qg8_ref[1]
    r = iota((FARK, HD), 0)
    mid = r - FAR8
    end = mid - 2 * FAR16
    back = jnp.where(r < FAR8, 1, jnp.where(end < 0, 2 + mid // FAR16, 4 + end // FAR32))
    spot = jnp.where(
        r < FAR8,
        r * 8 + rest8,
        jnp.where(end < 0, (mid % FAR16) * 16 + off % 16, (end % FAR32) * 32 + off % 32),
    )
    other = plane - back
    first = jnp.where(
        other < 0,
        9,
        jnp.where(other // 2 == plane // 2, 3, jnp.where(other // 4 == plane // 4, 4, 5)),
    )
    deep_q = depth_of(iota((8, FAR8), 1) * 8 + rest8, off)[:1]
    deep = jnp.minimum(deep_q, depth_of(spot, off))
    times = jnp.maximum(deep - first.astype(F32) + 1.0, 0.0)
    s = jnp.where(times > 0.0, nt(kf[...], qs) * C2, NEG)
    dp = nt(vf[...], gs)
    m_f = jnp.max(s, axis=0, keepdims=True)
    e = jnp.exp2(s - m_f)
    l_f = jnp.sum(e * times, axis=0, keepdims=True)
    d_f = jnp.sum(e.astype(BF16).astype(F32) * (dp * times), axis=0, keepdims=True)

    m_n, l_n, d_n = some_ref[0:1], some_ref[1:2], some_ref[2:3]
    m_s = jnp.maximum(m_n, m_f)
    fn = jnp.exp2(m_n - m_s)
    ff = jnp.exp2(m_f - m_s)
    l_s = l_n * fn + l_f * ff
    log_s = m_s + jnp.log2(l_s)
    dot_s = (d_n * fn + d_f * ff) / l_s
    near[...] = jnp.zeros((8, FAR8), F32)
    near[0:1] = log_s
    near[1:2] = dot_s
    wide = moved(near[...], every8(rest8), ((1,), (0,)))
    hit = (iota((8, ROW), 1) % 8 == rest8)[:1]
    fin_ref[...] = jnp.zeros((8, ROW), F32)
    total = stat_ref[1:2]
    fin_ref[0:1] = jnp.where(hit, wide[0:1], stat_ref[0:1] + jnp.log2(total))
    fin_ref[1:2] = jnp.where(hit, wide[1:2], stat_ref[2:3] / total)

    p = jnp.exp2(s - log_s) * times
    ds = (p * (dp - dot_s)).astype(BF16)
    dk = nn(ds, qs)
    dv = nn(p.astype(BF16), gs)
    dqf_ref[...] = tn(ds, kf[...])
    pf_ref[0] = dk[:FAR8]
    pf_ref[1] = dv[:FAR8]
    lo = FAR8
    for ref, size in ((h2_ref, FAR16), (h4_ref, FAR32), (h6_ref, FAR32)):
        for j in range(2):
            ref[j, 0] = dk[lo : lo + size].astype(BF16)
            ref[j, 1] = dv[lo : lo + size].astype(BF16)
            lo += size


def far_part(offsets, kv8, qg8, far, stat, some):
    out = [
        jax.ShapeDtypeStruct((8, ROW), F32),
        jax.ShapeDtypeStruct((2, 2, FAR16, HD), BF16),
        jax.ShapeDtypeStruct((2, 2, FAR32, HD), BF16),
        jax.ShapeDtypeStruct((2, 2, FAR32, HD), BF16),
        jax.ShapeDtypeStruct((FAR8, HD), F32),
        jax.ShapeDtypeStruct((2, FAR8, HD), F32),
    ]
    scratch = [
        pltpu.VMEM((FARK, HD), BF16),
        pltpu.VMEM((FARK, HD), BF16),
        pltpu.VMEM((8, FAR8), F32),
    ]
    return call(far_kernel, out, scratch, smem=(0,), nin=8)(
        offsets, kv8, qg8, *far, stat, some
    )


def back_prev_kernel(kv_ref, qg_ref, fin_ref, acc, ds_ref):
    plane, _ = place()
    there = plane > 0
    seen = iota((SLAB, SLAB), 0) > iota((SLAB, SLAB), 1)
    for kb in range(COLS):
        k = kv_ref[0, rows_of(kb)]
        v = kv_ref[1, rows_of(kb)]
        dk = jnp.zeros((SLAB, HD), F32)
        dv = jnp.zeros((SLAB, HD), F32)
        for qb in range(kb + 1):
            lanes = pl.ds(qb * SLAB, SLAB)
            q = qg_ref[0, rows_of(qb)]
            g = qg_ref[1, rows_of(qb)]
            log = jnp.where(there, fin_ref[0:1, lanes], -NEG)
            s = nt(k, q) * C2 - log
            if kb == qb:
                s = jnp.where(seen, s, NEG)
            p = jnp.exp2(s)
            ds = (p * (nt(v, g) - fin_ref[1:2, lanes])).astype(BF16)
            dv = dv + nn(p.astype(BF16), g)
            dk = dk + nn(ds, q)
            ds_ref[rows_of(kb), lanes] = ds
        acc[0, rows_of(kb)] = dk
        acc[1, rows_of(kb)] = dv


def back_prev(kv, qg, fin):
    out = [jax.ShapeDtypeStruct((2, ROW, HD), F32), jax.ShapeDtypeStruct((ROW, ROW), BF16)]
    return call(back_prev_kernel, out, nin=3)(kv, qg, fin)


def merge_kernel(off_ref, prev_ref, pf_ref, a2_ref, a4_ref, a6_ref, out_ref, acc):
    _, col = place()
    off = off_ref[col]
    every8th = pl.ds(off % 8, FAR8, stride=8)
    every16 = pl.ds(off % 16, FAR16, stride=16)
    every32 = pl.ds(off % 32, FAR32, stride=32)
    for which in range(2):
        acc[...] = prev_ref[which]
        acc[every8th, :] = acc[every8th, :] + pf_ref[which]
        acc[every16, :] = acc[every16, :] + a2_ref[1, which].astype(F32)
        acc[every32, :] = acc[every32, :] + (
            a4_ref[1, which].astype(F32) + a6_ref[1, which].astype(F32)
        )
        out_ref[which] = acc[...].astype(BF16)


def merge(offsets, prev, pf, a2, a4, a6):
    out = jax.ShapeDtypeStruct((2, ROW, HD), BF16)
    return call(merge_kernel, out, [pltpu.VMEM((ROW, HD), F32)], smem=(0,), nin=6)(
        offsets, prev, pf, a2, a4, a6
    )


def back_own_kernel(
    off_ref, kv_ref, qg_ref, fin_ref, tab_ref, prev_ref, ds_ref, dqf_ref, *refs
):
    own_ref, dq_ref, dq = refs
    _, col = place()
    strided = pl.ds(off_ref[col] % 8, FAR8, stride=8)
    seen = iota((SLAB, SLAB), 0) <= iota((SLAB, SLAB), 1)
    for qb in range(COLS):
        lanes = pl.ds(qb * SLAB, SLAB)
        q = qg_ref[0, rows_of(qb)]
        g = qg_ref[1, rows_of(qb)]
        dq_sum = tn(prev_ref[0, rows_of(qb)], ds_ref[rows_of(qb), lanes])
        for kb in range(qb + 1, COLS):
            dq_sum = dq_sum + tn(prev_ref[0, rows_of(kb)], ds_ref[rows_of(kb), lanes])
        for kb in range(qb + 1):
            k = kv_ref[0, rows_of(kb)]
            s = nt(k, q) * C2 - fin_ref[0:1, lanes]
            if kb == qb:
                s = jnp.where(seen, s, NEG)
            p = jnp.exp2(s) * tab_ref[int(kb // 2 == qb // 2)]
            ds = (p * (nt(kv_ref[1, rows_of(kb)], g) - fin_ref[1:2, lanes])).astype(BF16)
            dv = nn(p.astype(BF16), g)
            dk = nn(ds, q)
            dq_sum = dq_sum + tn(k, ds)
            if kb == qb:
                own_ref[0, rows_of(kb)] = dk
                own_ref[1, rows_of(kb)] = dv
            else:
                own_ref[0, rows_of(kb)] += dk
                own_ref[1, rows_of(kb)] += dv
        dq[rows_of(qb)] = dq_sum.T
    dq[strided, :] = dq[strided, :] + dqf_ref[...]
    dq_ref[...] = (dq[...] * SCALE).astype(BF16)


def back_own(offsets, kv, qg, fin, tab, prev, ds, dqf):
    out = [jax.ShapeDtypeStruct((2, ROW, HD), F32), jax.ShapeDtypeStruct((ROW, HD), BF16)]
    scratch = [pltpu.VMEM((ROW, HD), F32)]
    return call(back_own_kernel, out, scratch, smem=(0,), nin=8)(
        offsets, kv, qg, fin, tab, prev, ds, dqf
    )


def join_kernel(off_ref, dq_ref, own_ref, near_ref, a2_ref, a4_ref, a6_ref, *refs):
    out = refs[:COLS]
    acc = refs[COLS]
    _, col = place()
    off = off_ref[col]
    every16 = pl.ds(off % 16, FAR16, stride=16)
    every32 = pl.ds(off % 32, FAR32, stride=32)
    for which in range(2):
        acc[...] = own_ref[which] + near_ref[which].astype(F32)
        acc[every16, :] = acc[every16, :] + a2_ref[0, which].astype(F32)
        acc[every32, :] = acc[every32, :] + (
            a4_ref[0, which].astype(F32) + a6_ref[0, which].astype(F32)
        )
        for step in range(COLS):
            rows = pl.ds(pl.multiple_of(((col + step) % COLS) * SLAB, SLAB), SLAB)
            value = acc[rows]
            if which == 0:
                value = value * SCALE
                out[step][2] = dq_ref[rows]
            out[step][which] = value.astype(BF16)


def join(offsets, dq, own, near, a2, a4, a6):
    piece = jax.ShapeDtypeStruct((3, SLAB, HD), BF16)
    return call(
        join_kernel, [piece] * COLS, [pltpu.VMEM((ROW, HD), F32)], smem=(0,), nin=7
    )(offsets, dq, own, near, a2, a4, a6)


def spread_kernel(*refs):
    q_ref, k_ref, v_ref = refs[COLS:]
    _, col = place()
    for ref, step in zip(refs[:COLS], ORDER):
        lanes = pl.ds(pl.multiple_of(((col - step + COLS) % COLS) * HD, HD), HD)
        q_ref[:, lanes] = ref[2]
        k_ref[:, lanes] = ref[0]
        v_ref[:, lanes] = ref[1]


def spread(pieces):
    out = jax.ShapeDtypeStruct((SLAB, COLS * HD), BF16)
    return call(spread_kernel, [out] * 3, nin=COLS)(*[pieces[step] for step in ORDER])


def body(planes, query_states, key_states, value_states, out_grad, head_offsets):
    def exchange(pieces):
        return [pieces[0]] + [across(pieces[s], s, planes) for s in range(1, COLS)]

    kv = exchange(pack(key_states, value_states))
    qg = exchange(pack(query_states, out_grad))
    first = along(kv[0], 1, planes)
    first, *rest = lax.optimization_barrier((first, *[kv[step] for step in ORDER[1:]]))
    rest = along(stack(rest), 1, planes)
    row, mine_wide, mine_slim, tab = prepare(head_offsets, kv)
    prev, wide, slim = pair_up(head_offsets, mine_wide, mine_slim, first, rest)
    prev, qg[0] = lax.optimization_barrier((prev, qg[0]))
    stat_own, qg, qg8 = first_own(head_offsets, row, tab, qg)
    far = [along(wide, 2, planes), along(slim, 4, planes), along(slim, 6, planes)]
    stat, some, kv8 = first_prev(head_offsets, prev, qg, stat_own)
    fin, h2, h4, h6, dqf, pf = far_part(head_offsets, kv8, qg8, far, stat, some)
    a2, a4, a6 = [along(h, -step, planes) for h, step in ((h2, 2), (h4, 4), (h6, 6))]
    prev_grad, ds = back_prev(prev, qg, fin)
    near = along(merge(head_offsets, prev_grad, pf, a2, a4, a6), -1, planes)
    own, dq = back_own(head_offsets, row, qg, fin, tab, prev, ds, dqf)
    pieces = exchange(join(head_offsets, dq, own, near, a2, a4, a6))
    return tuple(spread(pieces))


def solution(mesh):
    spec = P(("batch", "seq"), "head")
    planes = mesh.shape["seq"] // COLS
    return jax.shard_map(
        functools.partial(body, planes),
        mesh=mesh,
        in_specs=(spec, spec, spec, spec, P("head")),
        out_specs=(spec, spec, spec),
        check_vma=False,
    )
```
